256 devices in a mesh: mode: 16 (over y_lo, x, core), elem: 16 (over z, y_hi).
Axes of the slice: x: 4, y: 4 (y_hi: 2, y_lo: 2; y = y_hi * 2 + y_lo), z: 8, core: 2. Of those that a mesh axis runs over, the one named last changes fastest.
Arguments:
- velocity: float32 [3, 128, 16384], P(None, 'mode', 'elem'), may hold values from -1.5 to 1.5
- metric_main: float32 [2, 16384], P(None, 'elem'), may hold values from 0.5 to 1.5
- metric_cross: float32 [2, 16384], P(None, 'elem'), may hold values from -0.5 to 0.5
- stiffness: float32 [16384, 512], P('elem'), as said below
- mass: float32 [16384], P('elem'), may hold values from 0.5 to 2
- precond: float32 [64, 16384, 512], P('mode', 'elem'), as said below
- trace_map: int32 [32, 2, 32], P('elem'), may hold values from 0 to 511, as said below
Outputs:
- new_velocity: float32 [3, 128, 16384], P(None, 'mode', 'elem')
The draws below stay inside these ranges and needn't reach their ends.
Inputs may be any that keep to these rules, and one draw needn't show every extreme that they name: trace_map[q, 0] and trace_map[q, 1] together hold 64 distinct points of patch q; slot j of trace_map[q, 1] and slot j of trace_map[q + 1, 0] are the same plane point. `stiffness`: each 512 x 512 block is symmetric. `precond`: one 512 x 512 matrix for each mode and patch.
All inputs are finite; a program needn't handle non-finite values.
Results may differ from the reference program's by a relative error of at most 0.0003.
Values sent between devices are 32-bit elements; how exact they have to be, the bound alone decides.
No kernel may reach another device: no remote copies, remote signals or barrier semaphores. Data moves between devices by JAX's collectives and lax.ppermute only.
A program may use at most 128 MiB of HBM per device.

```python
import math
import jax
import jax.numpy as jnp
import numpy as np
from jax import lax

MODES = 64
KZ = 128
NZ = 256
L = 512
TRACE = 32
NPATCH = 32
NPTS = 16384
STEPS = 4
ITERS = 4


def draw_stiffness(key, part):
    noise = jax.random.normal(jax.random.fold_in(key, 31), (NPATCH, L, L), jnp.float32)
    symmetric = (noise + jnp.swapaxes(noise, 1, 2)) * (0.5 / math.sqrt(2.0 * L))
    diagonal = jax.random.uniform(jax.random.fold_in(key, 32), (NPATCH, L, 1), jnp.float32, 1.0, 3.0)
    row_numbers = lax.broadcasted_iota(jnp.int32, (L, L), 0)
    column_numbers = lax.broadcasted_iota(jnp.int32, (L, L), 1)
    identity = (row_numbers == column_numbers).astype(jnp.float32)[None]
    blocks = symmetric * (1.0 - identity) + identity * diagonal
    return blocks.reshape(NPATCH * L, L)


def draw_precond(key, part):
    noise = jax.random.normal(jax.random.fold_in(key, 41), (MODES, NPATCH * L, L), jnp.float32)
    diagonal = jax.random.uniform(jax.random.fold_in(key, 42), (MODES, NPATCH * L, 1), jnp.float32, 0.8, 1.2)
    row_numbers = lax.broadcasted_iota(jnp.int32, (NPATCH * L, L), 0) % L
    column_numbers = lax.broadcasted_iota(jnp.int32, (NPATCH * L, L), 1)
    identity = (row_numbers == column_numbers).astype(jnp.float32)[None]
    wavenumber = 4.0 * jnp.arange(MODES, dtype=jnp.float32) / MODES
    mode_scale = 1.0 / (2.0 + 0.5 * wavenumber * wavenumber)
    return (identity * diagonal + 0.3 / math.sqrt(L) * noise) * mode_scale[:, None, None]


def draw_trace_map(key, part):
    patch_keys = jax.random.split(jax.random.fold_in(key, 51), NPATCH)
    scores = jax.vmap(lambda patch_key: jax.random.permutation(patch_key, L))(patch_keys).astype(jnp.int32)
    first_patch = (jnp.arange(NPATCH, dtype=jnp.int32) == 0)[:, None]
    position = jnp.arange(L, dtype=jnp.int32)[None, :]
    scores = jnp.where(first_patch & (position == L - 1), -2, scores)
    scores = jnp.where(first_patch & (position == 0), -1, scores)
    ordering = jnp.argsort(scores, axis=1, stable=True).astype(jnp.int32)
    return ordering[:, :2 * TRACE].reshape(NPATCH, 2, TRACE)


def level_of(own_key, extent, pieces, smallest, high):
    def one(dim, shards_of):
        heights = jax.random.uniform(jax.random.fold_in(jax.random.fold_in(own_key, 6), dim), (shards_of,), jnp.float32, smallest / len(pieces), high / len(pieces))
        return jnp.repeat(jnp.exp(heights), extent[dim] // shards_of).reshape((-1,) + (1,) * (len(extent) - dim - 1))

    gain = one(*pieces[0])
    for cut in pieces[1:]:
        gain = gain * one(*cut)
    return gain


def bell_draw(key, dims, scale, most, cuts=(), kind=jnp.bfloat16):
    array = scale * jax.random.normal(key, dims, jnp.float32)
    if cuts:
        array = array * level_of(key, dims, cuts, -0.22, 0.18)
    return jnp.clip(array, -most, most).astype(kind)


def setup_inputs(seed: int = 0) -> dict:
    key_list = jax.random.split(jax.random.key(seed), 8)
    velocity = bell_draw(key_list[0], (3, KZ, NPTS), 0.25, 1.5, ((1, 16), (2, 16)), jnp.float32)
    metric_main = jnp.clip(0.5 + 1.0 * jax.random.uniform(key_list[1], (2, NPTS), jnp.float32) ** level_of(key_list[1], (2, NPTS), ((1, 16),), -0.2, 0.2), 0.5, 1.5)
    metric_cross = jnp.clip(jax.random.uniform(key_list[2], (2, NPTS), jnp.float32, -0.5, 0.5) * level_of(key_list[2], (2, NPTS), ((1, 16),), -0.4, 0.0), -0.5, 0.5)
    stiffness = draw_stiffness(jax.random.fold_in(key_list[7], 71), 0)
    mass = jnp.clip(jnp.exp(math.log(2.0) - 1.3862944 * jax.random.uniform(key_list[4], (NPATCH * L,), jnp.float32) ** level_of(key_list[4], (NPATCH * L,), ((0, 16),), -0.2, 0.2)), 0.5, 2.0)
    precond = draw_precond(jax.random.fold_in(key_list[7], 71), 0)
    trace_map = draw_trace_map(jax.random.fold_in(key_list[7], 71), 0)
    return {"velocity": velocity, "metric_main": metric_main, "metric_cross": metric_cross, "stiffness": stiffness, "mass": mass, "precond": precond, "trace_map": trace_map}


highest_precision = lax.Precision.HIGHEST
viscous_step = 0.5
time_step = 0.02
relaxation = 0.8


def chebyshev_matrix():
    node_points = np.cos(np.pi * np.arange(8) / 7.0)
    weights = np.where((np.arange(8) == 0) | (np.arange(8) == 7), 2.0, 1.0)
    parity = np.where((np.arange(8)[:, None] + np.arange(8)[None, :]) % 2 == 0, 1.0, -1.0)
    identity = np.eye(8)
    spacing = node_points[:, None] - node_points[None, :] + identity
    off_diagonal = (weights[:, None] / weights[None, :]) * parity / spacing * (1.0 - identity)
    return off_diagonal - identity * off_diagonal.sum(axis=1)[:, None]


def spanwise_tables():
    spanwise = jnp.arange(NZ, dtype=jnp.int32)
    row_numbers = jnp.arange(KZ, dtype=jnp.int32)
    wavenumber = row_numbers // 2
    product = (spanwise[:, None] * wavenumber[None, :]) % NZ
    phase_angle = (2.0 * math.pi / NZ) * product.astype(jnp.float32)
    is_sine = (row_numbers % 2 == 1)[None, :]
    basis_table = jnp.where(is_sine, jnp.sin(phase_angle), jnp.cos(phase_angle))
    wave_rate = 4.0 * wavenumber.astype(jnp.float32) / MODES
    slope_table = jnp.where(is_sine, wave_rate[None, :] * jnp.cos(phase_angle), -wave_rate[None, :] * jnp.sin(phase_angle))
    norm_factor = jnp.where(row_numbers == 0, 1.0 / NZ, 2.0 / NZ).astype(jnp.float32)
    forward = basis_table.T * norm_factor[:, None]
    return basis_table, slope_table, forward, wave_rate


def reference(velocity, metric_main, metric_cross, stiffness, mass, precond, trace_map):
    chebyshev = jnp.asarray(chebyshev_matrix(), jnp.float32)
    basis_table, slope_table, forward, wave_rate = spanwise_tables()
    wave_modes = wave_rate.reshape(MODES, 2)[:, 0]
    damping = (1.0 + viscous_step * wave_rate * wave_rate)[None, :, None, None]
    patches = stiffness.reshape(NPATCH, L, L)
    patch_mass = mass.reshape(NPATCH, L)
    inverse = precond.reshape(MODES, NPATCH, L, L)
    left_trace = trace_map[:, 0]
    right_trace = trace_map[:, 1]
    patch_rows = jnp.arange(NPATCH)[:, None]
    patch_numbers = jnp.arange(NPATCH)
    left_gain = jnp.broadcast_to((patch_numbers > 0)[:, None], left_trace.shape).astype(jnp.float32)
    right_gain = jnp.broadcast_to((patch_numbers < NPATCH - 1)[:, None], right_trace.shape).astype(jnp.float32)
    multiplicity = jnp.ones((NPATCH, L), jnp.float32).at[patch_rows, left_trace].add(left_gain).at[patch_rows, right_trace].add(right_gain)
    weight = relaxation / (multiplicity * multiplicity)

    def assemble(values):
        left_values = values[:, :, patch_rows, left_trace]
        right_values = values[:, :, patch_rows, right_trace]
        nothing = jnp.zeros_like(left_values[:, :, :1])
        from_below = jnp.concatenate([nothing, right_values[:, :, :-1]], axis=2)
        from_above = jnp.concatenate([left_values[:, :, 1:], nothing], axis=2)
        return values.at[:, :, patch_rows, left_trace].add(from_below).at[:, :, patch_rows, right_trace].add(from_above)

    state = velocity
    for time_level in range(STEPS):
        element_view = state.reshape(3, KZ, NPTS // 64, 8, 8)
        xi_slope = jnp.einsum("creyj,xj->creyx", element_view, chebyshev, precision=highest_precision).reshape(state.shape)
        eta_slope = jnp.einsum("crejx,yj->creyx", element_view, chebyshev, precision=highest_precision).reshape(state.shape)
        grad_x = metric_main[0] * xi_slope + metric_cross[0] * eta_slope
        grad_y = metric_cross[1] * xi_slope + metric_main[1] * eta_slope
        pairs = state.reshape(3, MODES, 2, NPTS)
        grad_z = jnp.stack([wave_modes[None, :, None] * pairs[:, :, 1], -wave_modes[None, :, None] * pairs[:, :, 0]], axis=2).reshape(state.shape)
        fields = jnp.concatenate([state, grad_x, grad_y, grad_z], axis=0)
        physical = jnp.einsum("frp,zr->fpz", fields, basis_table, precision=highest_precision)
        advection = physical[0:1] * physical[3:6] + physical[1:2] * physical[6:9] + physical[2:3] * physical[9:12]
        advection_hat = jnp.einsum("ipz,rz->irp", advection, forward, precision=highest_precision)
        source = (state - time_step * advection_hat).reshape(3, KZ, NPATCH, L)
        local_term = patch_mass * source
        iterate = jnp.zeros_like(source)
        for sweep_number in range(ITERS):
            if sweep_number == 0:
                residual = assemble(local_term)
            else:
                stiff_part = jnp.einsum("pij,crpj->crpi", patches, iterate, precision=highest_precision)
                residual = assemble(local_term - viscous_step * stiff_part - damping * patch_mass * iterate)
            grouped = residual.reshape(3, MODES, 2, NPATCH, L)
            correction = jnp.einsum("kpij,ckhpj->ckhpi", inverse, grouped, precision=highest_precision).reshape(3, KZ, NPATCH, L)
            iterate = iterate + weight * assemble(correction)
        state = iterate.reshape(3, KZ, NPTS)
    return state
```

```python
import functools
import math

import jax
import jax.numpy as jnp
import numpy as np
from jax import lax
from jax.experimental import pallas as pl
from jax.experimental.pallas import tpu as pltpu
from jax.sharding import PartitionSpec as P

MODES = 64
KZ = 128
NZ = 256
STEPS = 4
ITERS = 4
SLOT = 8

viscous_step = 0.5
time_step = 0.02
relaxation = 0.8

f32 = jnp.float32
bf16 = jnp.bfloat16


def chebyshev_matrix():
    node_points = np.cos(np.pi * np.arange(8) / 7.0)
    weights = np.where((np.arange(8) == 0) | (np.arange(8) == 7), 2.0, 1.0)
    parity = np.where((np.arange(8)[:, None] + np.arange(8)[None, :]) % 2 == 0, 1.0, -1.0)
    identity = np.eye(8)
    spacing = node_points[:, None] - node_points[None, :] + identity
    off_diagonal = weights[:, None] / weights[None, :] * parity / spacing * (1.0 - identity)
    return off_diagonal - identity * off_diagonal.sum(axis=1)[:, None]


def halves(table):
    table = np.asarray(table, np.float32)
    high = table.astype(bf16)
    low = (table - high.astype(np.float32)).astype(bf16)
    return high, low


def spanwise_tables():
    rows = np.arange(KZ)
    wavenumber = rows // 2
    product = (np.arange(NZ)[:, None] * wavenumber[None, :]) % NZ
    phase = 2.0 * math.pi / NZ * product
    sine = (rows % 2 == 1)[None, :]
    rate = 4.0 * wavenumber / MODES
    basis = np.where(sine, np.sin(phase), np.cos(phase))
    slope = np.where(sine, rate * np.cos(phase), -rate * np.sin(phase))
    forward = basis.T * np.where(rows == 0, 1.0 / NZ, 2.0 / NZ)[:, None]

    def left(table):
        high, low = halves(table)
        return np.concatenate([high, low, high], axis=1)

    return left(basis), left(slope), left(forward)


def slope_weights():
    chebyshev = chebyshev_matrix()
    along_xi = np.kron(np.eye(8), chebyshev.T)
    along_eta = np.kron(chebyshev.T, np.eye(8))
    both = np.concatenate([np.kron(np.eye(2), along_xi), np.kron(np.eye(2), along_eta)], axis=1)
    high, low = halves(both)
    return np.stack([high, low])


def split(value):
    high = value.astype(bf16).astype(f32)
    return high, value - high


def stacked(value):
    return jnp.concatenate(split(value), axis=0).astype(bf16)


def folded(value):
    half = value.shape[0] // 2
    return value[:half] + value[half:]


def dot(a, b):
    return jnp.dot(a, b, preferred_element_type=f32)


def lanes(shape):
    return lax.broadcasted_iota(jnp.int32, shape, len(shape) - 1)


def pick(value, chooser):
    return folded(dot(stacked(value), chooser))


def scatter(trace, spreader):
    high, low = split(trace)
    return dot((high + pltpu.roll(low, 64, 1)).astype(bf16), spreader)


def thin(trace, table):
    return folded(dot(stacked(trace + pltpu.roll(trace, 64, 1)), table))


def mode_rows(value, k):
    return value[SLOT * k : SLOT * (k + 1)]


def pack_points(fields, send_ref):
    first_half = lanes((8, 128)) < 64
    for t in range(8):
        c0, c1, c2 = [fields[c][:, 128 * t : 128 * (t + 1)] for c in range(3)]
        send_ref[2 * t, 0] = jnp.where(first_half, c0, pltpu.roll(c1, 64, 1))
        send_ref[2 * t + 1, 0] = jnp.where(first_half, pltpu.roll(c0, 64, 1), c1)
        send_ref[2 * t, 1] = jnp.where(first_half, c2, 0.0)
        send_ref[2 * t + 1, 1] = jnp.where(first_half, pltpu.roll(c2, 64, 1), 0.0)


def start_kernel(velocity_ref, send_ref, state_ref):
    pack_points([velocity_ref[c] for c in range(3)], send_ref)
    state_ref[...] = jnp.zeros_like(state_ref)
    width = state_ref.shape[2]
    for q in range(state_ref.shape[0]):
        for k in range(4):
            for c in range(3):
                state_ref[q, SLOT * k + 2 * c : SLOT * k + 2 * c + 2, :] = velocity_ref[
                    c, 2 * k : 2 * k + 2, width * q : width * (q + 1)
                ]


def advection_kernel(seen_ref, metric_ref, slopes_ref, basis_ref, slope_ref, forward_ref, send_ref):
    first_half = lanes((KZ, 128)) < 64
    field01 = seen_ref[:, 0].reshape(KZ, 128)
    field2 = seen_ref[:, 1].reshape(KZ, 128)
    both = jnp.concatenate([field01, field2], axis=0)
    rows = stacked(both)
    slopes = folded(dot(rows, slopes_ref[0]) + dot(rows, slopes_ref[1]))
    xi, eta = slopes[:, :128], slopes[:, 128:]
    grad_x = metric_ref[0:1] * xi + metric_ref[2:3] * eta
    grad_y = metric_ref[3:4] * xi + metric_ref[1:2] * eta
    turned01 = pltpu.roll(field01, 64, 1)
    speed_u = jnp.where(first_half, field01, turned01)
    speed_v = jnp.where(first_half, turned01, field01)
    speed_w = jnp.where(first_half, field2, pltpu.roll(field2, 64, 1))

    def right(value):
        high, low = split(value)
        high = high.astype(bf16)
        return jnp.concatenate([high, high, low.astype(bf16)], axis=0)

    def physical(table_ref, value):
        return dot(table_ref[...], right(value))

    speeds = [physical(basis_ref, value) for value in (speed_u, speed_v, speed_w)]
    for part in range(2):
        keep = slice(KZ * part, KZ * (part + 1))
        advection = (
            speeds[0] * physical(basis_ref, grad_x[keep])
            + speeds[1] * physical(basis_ref, grad_y[keep])
            + speeds[2] * physical(slope_ref, both[keep])
        )
        send_ref[:, part] = dot(forward_ref[...], right(advection)).reshape(16, 8, 128)


def table_kernel(
    precond_ref, chooser_ref, spreader_ref, inverse_ref, column_ref, corner_ref, link_ref
):
    step = pl.program_id(0)
    q = lax.rem(step, 2)
    k = lax.div(step, 2)
    turned = precond_ref[0].T
    high = turned.astype(bf16)
    low = (turned - high.astype(f32)).astype(bf16)
    inverse_ref[step, 0] = high
    inverse_ref[step, 1] = low
    spreader = spreader_ref[q, 0:64]
    column_high = dot(spreader, high).astype(bf16)
    column_low = dot(spreader, low).astype(bf16)
    column_ref[step, 0:64] = column_high
    column_ref[step, 64:128] = column_low
    chooser = chooser_ref[q]
    corner = dot(column_high, chooser) + dot(column_low, chooser)
    corner_high = corner.astype(bf16)
    corner_ref[step, 0:64] = corner_high
    corner_ref[step, 64:128] = (corner - corner_high.astype(f32)).astype(bf16)

    @pl.when(q == 0)
    def _():
        link_ref[0, k] = corner[0:32]

    @pl.when(q == 1)
    def _():
        link_ref[1, k] = corner[32:64]


def link_kernel(lower_ref, upper_ref, gate_ref, stiffness_ref, link_ref, stiff_ref):
    for k in range(lower_ref.shape[0]):
        table = jnp.concatenate([upper_ref[k] * gate_ref[1:2], lower_ref[k] * gate_ref[0:1]], axis=0)
        high, low = split(table)
        link_ref[k, 0:64] = high.astype(bf16)
        link_ref[k, 64:128] = low.astype(bf16)
    width = stiff_ref.shape[2]
    for q in range(stiff_ref.shape[0]):
        high, low = split(viscous_step * stiffness_ref[width * q : width * (q + 1)])
        stiff_ref[q, 0] = high.astype(bf16)
        stiff_ref[q, 1] = low.astype(bf16)


def precondition(residual, inverse_ref, chooser_ref, spreader_ref, outs):
    part_ref, trace_ref, up_ref, down_ref = outs
    lane = lanes((32, 128))
    trace = [pick(residual[q], chooser_ref[q]) for q in range(2)]
    gained = [
        residual[0] + scatter(jnp.where((lane >= 32) & (lane < 64), trace[1], 0.0), spreader_ref[0]),
        residual[1] + scatter(jnp.where(lane < 32, trace[0], 0.0), spreader_ref[1]),
    ]
    for q in range(2):
        high, low = split(gained[q])
        parts = []
        for k in range(4):
            rows = jnp.concatenate([mode_rows(high, k), mode_rows(low, k)], axis=0).astype(bf16)
            parts.append(
                folded(dot(rows, inverse_ref[2 * k + q, 0]) + dot(rows, inverse_ref[2 * k + q, 1]))
            )
        part = jnp.concatenate(parts, axis=0)
        part_ref[q] = part
        part_trace = pick(part, chooser_ref[q])
        message = trace[q] + pltpu.roll(part_trace, 64, 1)
        trace_ref[q] = message
        if q == 0:
            down_ref[...] = message
        else:
            up_ref[...] = message


def first_kernel(
    seen_ref, state_ref, mass_ref, inverse_ref, chooser_ref, spreader_ref,
    local_ref, part_ref, trace_ref, up_ref, down_ref,
):
    first_half = lanes((8, 128)) < 64
    local_ref[...] = jnp.zeros_like(local_ref)
    per_patch = local_ref.shape[2] // 128
    for t in range(8):
        a0, b0 = seen_ref[2 * t, 0], seen_ref[2 * t + 1, 0]
        a1, b1 = seen_ref[2 * t, 1], seen_ref[2 * t + 1, 1]
        fields = [
            jnp.where(first_half, a0, pltpu.roll(b0, 64, 1)),
            jnp.where(first_half, pltpu.roll(a0, 64, 1), b0),
            jnp.where(first_half, a1, pltpu.roll(b1, 64, 1)),
        ]
        where = slice(128 * (t % per_patch), 128 * (t % per_patch + 1))
        for k in range(4):
            for c in range(3):
                local_ref[t // per_patch, SLOT * k + 2 * c : SLOT * k + 2 * c + 2, where] = fields[c][
                    2 * k : 2 * k + 2
                ]
    local = [mass_ref[q] * (state_ref[q] - time_step * local_ref[q]) for q in range(2)]
    for q in range(2):
        local_ref[q] = local[q]
    precondition(local, inverse_ref, chooser_ref, spreader_ref, (part_ref, trace_ref, up_ref, down_ref))


def update(
    lower_ref, upper_ref, part_ref, trace_ref, gate_ref, weight_ref, column_ref, corner_ref, link_ref,
    spreader_ref,
):
    lane = lanes((32, 128))
    lower_gate = (lane < 32) & (gate_ref[0:1] > 0.0)
    upper_gate = (lane >= 32) & (lane < 64) & (gate_ref[1:2] > 0.0)
    lower, upper = lower_ref[...], upper_ref[...]
    inflow = [jnp.where(lower_gate, lower, 0.0), jnp.where(upper_gate, upper, 0.0)]
    lower_turned, upper_turned = pltpu.roll(lower, 64, 1), pltpu.roll(upper, 64, 1)
    own = [trace_ref[q] for q in range(2)]
    own_trace = [jnp.where(lane < 64, own[q], 0.0) for q in range(2)]
    own_part = [jnp.where(lane < 64, pltpu.roll(own[q], 64, 1), 0.0) for q in range(2)]
    added, full_trace, linked = [], [], []
    for q in range(2):
        added.append(
            jnp.concatenate([thin(mode_rows(inflow[q], k), column_ref[2 * k + q]) for k in range(4)], axis=0)
        )
        full_trace.append(
            own_part[q]
            + jnp.concatenate([thin(mode_rows(inflow[q], k), corner_ref[2 * k + q]) for k in range(4)], axis=0)
        )
        linked.append(
            jnp.concatenate([thin(mode_rows(own_trace[q], k), link_ref[k]) for k in range(4)], axis=0)
        )
    inner = (lane >= 32) & (lane < 64)
    gains = [
        jnp.where(lower_gate, lower_turned + linked[0], 0.0) + jnp.where(inner, full_trace[1], 0.0),
        jnp.where(upper_gate, upper_turned + linked[1], 0.0) + jnp.where(lane < 32, full_trace[0], 0.0),
    ]
    return [
        weight_ref[q] * (part_ref[q] + added[q] + scatter(gains[q], spreader_ref[q])) for q in range(2)
    ]


def sweep_kernel(
    fresh, *refs
):
    refs = list(refs)
    lower_ref, upper_ref, part_ref, trace_ref, local_ref = refs[:5]
    refs = refs[5:]
    if not fresh:
        iterate_ref, refs = refs[0], refs[1:]
    (
        gate_ref, weight_ref, column_ref, corner_ref, link_ref, spreader_ref, chooser_ref, damped_ref,
        stiff_ref, inverse_ref, next_ref, part_out, trace_out, up_ref, down_ref,
    ) = refs
    step = update(
        lower_ref, upper_ref, part_ref, trace_ref, gate_ref, weight_ref, column_ref, corner_ref,
        link_ref, spreader_ref,
    )
    residual = []
    for q in range(2):
        iterate = step[q] if fresh else iterate_ref[q] + step[q]
        next_ref[q] = iterate
        rows = stacked(iterate)
        stiff = folded(dot(rows, stiff_ref[q, 0]) + dot(rows, stiff_ref[q, 1]))
        residual.append(local_ref[q] - stiff - damped_ref[q] * iterate)
    precondition(residual, inverse_ref, chooser_ref, spreader_ref, (part_out, trace_out, up_ref, down_ref))


def last_kernel(
    final, lower_ref, upper_ref, part_ref, trace_ref, iterate_ref, gate_ref, weight_ref, column_ref,
    corner_ref, link_ref, spreader_ref, *outs
):
    step = update(
        lower_ref, upper_ref, part_ref, trace_ref, gate_ref, weight_ref, column_ref, corner_ref,
        link_ref, spreader_ref,
    )
    state = [iterate_ref[q] + step[q] for q in range(2)]
    field_ref = outs[0] if final else outs[2]
    width = state[0].shape[1]
    for q in range(2):
        for k in range(4):
            for c in range(3):
                field_ref[c, 2 * k : 2 * k + 2, width * q : width * (q + 1)] = state[q][
                    SLOT * k + 2 * c : SLOT * k + 2 * c + 2
                ]
    if not final:
        send_ref, state_ref = outs[0], outs[1]
        for q in range(2):
            state_ref[q] = state[q]
        pack_points([field_ref[c] for c in range(3)], send_ref)


VMEM = pl.BlockSpec(memory_space=pltpu.VMEM)


def call(kernel, outs, *args, scratch=(), name=None, flops=0):
    single = not isinstance(outs, (list, tuple))
    shapes = [outs] if single else list(outs)
    return pl.pallas_call(
        kernel,
        out_shape=shapes[0] if single else shapes,
        in_specs=[VMEM] * len(args),
        out_specs=VMEM if single else [VMEM] * len(shapes),
        scratch_shapes=list(scratch),
        name=name,
        compiler_params=pltpu.CompilerParams(vmem_limit_bytes=24 << 20),
    )(*args)


def shape(*dims, dtype=f32):
    return jax.ShapeDtypeStruct(dims, dtype)


def on_device(velocity, metric_main, metric_cross, stiffness, mass, precond, trace_map):
    points = velocity.shape[2]
    width = stiffness.shape[1]
    patches = trace_map.shape[0]
    mode_count = lax.axis_size("mode")
    elem_count = lax.axis_size("elem")
    mode_index = lax.axis_index("mode")
    elem_index = lax.axis_index("elem")
    share = points // mode_count

    traces = trace_map.reshape(patches, -1)
    swapped = jnp.concatenate([trace_map[:, 1], trace_map[:, 0]], axis=1)
    nowhere = jnp.full_like(traces, -1)
    places = jnp.arange(width, dtype=jnp.int32)
    spreader = (jnp.concatenate([traces, traces], axis=1)[:, :, None] == places).astype(bf16)
    chooser = (
        jnp.concatenate([swapped, nowhere], axis=1)[:, None, :] == places[None, :, None]
    ).astype(bf16)
    global_patch = elem_index * patches + jnp.arange(patches)
    lower_gain = (global_patch > 0)[:, None]
    upper_gain = (global_patch < patches * elem_count - 1)[:, None]
    lower_hit = jnp.any(trace_map[:, 0][:, :, None] == places, axis=1) & lower_gain
    upper_hit = jnp.any(trace_map[:, 1][:, :, None] == places, axis=1) & upper_gain
    multiplicity = 1.0 + lower_hit.astype(f32) + upper_hit.astype(f32)
    weight = (relaxation / (multiplicity * multiplicity))[:, None, :]
    lane = jnp.arange(128)
    gate = jnp.stack(
        [
            ((lane < 32) & (elem_index > 0)).astype(f32),
            ((lane >= 32) & (lane < 64) & (elem_index < elem_count - 1)).astype(f32),
        ]
    )
    patch_mass = mass.reshape(patches, 1, width)
    wave = 4.0 * (mode_index * 4 + jnp.arange(4)).astype(f32) / MODES
    damping = jnp.repeat(1.0 + viscous_step * wave * wave, SLOT)[None, :, None]
    damped = damping * patch_mass
    metric = lax.dynamic_slice_in_dim(
        jnp.concatenate([metric_main, metric_cross], axis=0), mode_index * share, share, axis=1
    )
    metric = jnp.concatenate([metric, metric], axis=1)
    basis, slope, forward = [jnp.asarray(table) for table in spanwise_tables()]
    slopes = jnp.asarray(slope_weights())

    packed = shape(16, 2, 8, 128)
    solver = shape(2, 32, width)
    trace_pair = shape(2, 32, 128)
    message = shape(32, 128)
    send, state = call(start_kernel, [packed, solver], velocity, name="start")

    inverse, column, corner, links = pl.pallas_call(
        table_kernel,
        grid=(8,),
        out_shape=[
            shape(8, 2, width, width, dtype=bf16),
            shape(8, 128, width, dtype=bf16),
            shape(8, 128, 128, dtype=bf16),
            shape(2, 4, 32, 128),
        ],
        in_specs=[
            pl.BlockSpec((1, width, width), lambda i: (i // 2, i % 2, 0)),
            VMEM,
            VMEM,
        ],
        out_specs=[VMEM] * 4,
        name="tables",
        compiler_params=pltpu.CompilerParams(vmem_limit_bytes=24 << 20),
    )(precond, chooser, spreader)

    up = [(i, (i + 1) % elem_count) for i in range(elem_count)]
    down = [((i + 1) % elem_count, i) for i in range(elem_count)]

    def neighbours(upward, downward):
        return lax.ppermute(upward, "elem", up), lax.ppermute(downward, "elem", down)

    lower_link, upper_link = neighbours(links[1], links[0])
    link, stiff = call(
        link_kernel,
        [shape(4, 128, 128, dtype=bf16), shape(2, 2, width, width, dtype=bf16)],
        lower_link, upper_link, gate, stiffness, name="links",
    )

    def transpose(value):
        return lax.all_to_all(value, "mode", split_axis=0, concat_axis=0, tiled=True)

    shared = (gate, weight, column, corner, link, spreader)
    for time_level in range(STEPS):
        send = call(
            advection_kernel, packed, transpose(send), metric, slopes, basis, slope, forward, name="advection"
        )
        local, part, trace, upward, downward = call(
            first_kernel, [solver, solver, trace_pair, message, message],
            transpose(send), state, patch_mass, inverse, chooser, spreader, name="first",
        )
        iterate = None
        for sweep_number in range(1, ITERS):
            lower, upper = neighbours(upward, downward)
            fresh = iterate is None
            iterate, part, trace, upward, downward = call(
                functools.partial(sweep_kernel, fresh),
                [solver, solver, trace_pair, message, message],
                lower, upper, part, trace, local, *(() if fresh else (iterate,)), *shared,
                chooser, damped, stiff, inverse, name="sweep",
            )
        lower, upper = neighbours(upward, downward)
        field = shape(3, 8, points)
        args = (lower, upper, part, trace, iterate, *shared)
        if time_level < STEPS - 1:
            send, state = call(
                functools.partial(last_kernel, False), [packed, solver], *args,
                scratch=[pltpu.VMEM((3, 8, points), f32)], name="last",
            )
        else:
            state = call(functools.partial(last_kernel, True), field, *args, name="final")
    return state


def solution(mesh):
    return jax.shard_map(
        on_device,
        mesh=mesh,
        in_specs=(
            P(None, "mode", "elem"),
            P(None, "elem"),
            P(None, "elem"),
            P("elem", None),
            P("elem"),
            P("mode", "elem", None),
            P("elem", None, None),
        ),
        out_specs=P(None, "mode", "elem"),
        check_vma=False,
    )
```

```python
import functools
import math

import jax
import jax.numpy as jnp
import numpy as np
from jax import lax
from jax.experimental import pallas as pl
from jax.experimental.pallas import tpu as pltpu
from jax.sharding import PartitionSpec as P

MODES = 64
KZ = 128
NZ = 256
STEPS = 4
ITERS = 4
TRACE = 32
SLOT = 8

viscous_step = 0.5
time_step = 0.02
relaxation = 0.8

f32 = jnp.float32
bf16 = jnp.bfloat16


def chebyshev_matrix():
    node_points = np.cos(np.pi * np.arange(8) / 7.0)
    weights = np.where((np.arange(8) == 0) | (np.arange(8) == 7), 2.0, 1.0)
    parity = np.where((np.arange(8)[:, None] + np.arange(8)[None, :]) % 2 == 0, 1.0, -1.0)
    identity = np.eye(8)
    spacing = node_points[:, None] - node_points[None, :] + identity
    off_diagonal = weights[:, None] / weights[None, :] * parity / spacing * (1.0 - identity)
    return off_diagonal - identity * off_diagonal.sum(axis=1)[:, None]


def halves(table):
    table = np.asarray(table, np.float32)
    high = table.astype(bf16)
    low = (table - high.astype(np.float32)).astype(bf16)
    return high, low


def spanwise_tables():
    rows = np.arange(KZ)
    wavenumber = rows // 2
    product = (np.arange(NZ)[:, None] * wavenumber[None, :]) % NZ
    phase = 2.0 * math.pi / NZ * product
    sine = (rows % 2 == 1)[None, :]
    rate = 4.0 * wavenumber / MODES
    basis = np.where(sine, np.sin(phase), np.cos(phase))
    slope = np.where(sine, rate * np.cos(phase), -rate * np.sin(phase))
    forward = basis.T * np.where(rows == 0, 1.0 / NZ, 2.0 / NZ)[:, None]

    def left(table):
        high, low = halves(table)
        return np.concatenate([high, low, high], axis=1)

    return left(basis), left(slope), left(forward)


def slope_weights():
    chebyshev = chebyshev_matrix()
    along_xi = np.kron(np.eye(8), chebyshev.T)
    along_eta = np.kron(chebyshev.T, np.eye(8))
    both = np.concatenate([np.kron(np.eye(2), along_xi), np.kron(np.eye(2), along_eta)], axis=1)
    high, low = halves(both)
    return np.stack([high, low])


def split(value):
    high = value.astype(bf16).astype(f32)
    return high, value - high


def stacked(value):
    return jnp.concatenate(split(value), axis=0).astype(bf16)


def folded(value):
    half = value.shape[0] // 2
    return value[:half] + value[half:]


def dot(a, b):
    return jnp.dot(a, b, preferred_element_type=f32)


def lanes(shape):
    return lax.broadcasted_iota(jnp.int32, shape, len(shape) - 1)


def pick(value, chooser):
    return folded(dot(stacked(value), chooser))


def scatter(trace, spreader):
    high, low = split(trace)
    return dot((high + pltpu.roll(low, 64, 1)).astype(bf16), spreader)


def both(value, table_ref):
    rows = stacked(value)
    return folded(dot(rows, table_ref[0]) + dot(rows, table_ref[1]))


def mode_rows(value, k):
    return value[SLOT * k : SLOT * (k + 1)]


def turned(value, start, stop):
    parts = []
    for k in range(4):
        by = (stop(k) - start(k)) % 128
        rows = mode_rows(value, k)
        parts.append(pltpu.roll(rows, by, 1) if by else rows)
    return jnp.concatenate(parts, axis=0)


def own_block():
    return lanes((32, 128)) // TRACE == lax.broadcasted_iota(jnp.int32, (32, 128), 0) // SLOT


def blocked(value, lane):
    return jnp.where(own_block(), turned(value, lambda k: lane, lambda k: TRACE * k), 0.0)


def unblocked(value, lane):
    return turned(jnp.where(own_block(), value, 0.0), lambda k: TRACE * k, lambda k: lane)


def pack_points(fields, send_ref):
    first_half = lanes((8, 128)) < 64
    for t in range(8):
        c0, c1, c2 = [fields[c][:, 128 * t : 128 * (t + 1)] for c in range(3)]
        send_ref[2 * t, 0] = jnp.where(first_half, c0, pltpu.roll(c1, 64, 1))
        send_ref[2 * t + 1, 0] = jnp.where(first_half, pltpu.roll(c0, 64, 1), c1)
        send_ref[2 * t, 1] = jnp.where(first_half, c2, 0.0)
        send_ref[2 * t + 1, 1] = jnp.where(first_half, pltpu.roll(c2, 64, 1), 0.0)


def start_kernel(velocity_ref, send_ref, state_ref):
    pack_points([velocity_ref[c] for c in range(3)], send_ref)
    state_ref[...] = jnp.zeros_like(state_ref)
    width = state_ref.shape[2]
    for q in range(state_ref.shape[0]):
        for k in range(4):
            for c in range(3):
                state_ref[q, SLOT * k + 2 * c : SLOT * k + 2 * c + 2, :] = velocity_ref[
                    c, 2 * k : 2 * k + 2, width * q : width * (q + 1)
                ]


def setup_kernel(
    index_ref, maps_ref, mass_ref, main_ref, cross_ref, slopes_ref, basis_ref, slope_ref, forward_ref,
    spreader_ref, chooser_ref, lane_chooser_ref, weight_ref, gate_ref, row_mass_ref, damped_ref, metric_ref,
    slopes_out, basis_out, slope_out, forward_out,
):
    mode, elem, last = index_ref[0], index_ref[1], index_ref[2]
    width = spreader_ref.shape[2]
    lower = jnp.where(elem > 0, 1.0, 0.0)
    upper = jnp.where(elem < last, 1.0, 0.0)
    gate_ref[0:1] = jnp.full((1, 128), lower, f32)
    gate_ref[1:2] = jnp.full((1, 128), upper, f32)
    diagonal = lax.broadcasted_iota(jnp.int32, (128, 128), 0) == lanes((128, 128))
    across = lanes((128, width)).astype(f32)
    along = lax.broadcasted_iota(jnp.int32, (width, 128), 0).astype(f32)
    rows = lax.broadcasted_iota(jnp.int32, (32, width), 0) // SLOT + 4 * mode
    wave = (4.0 / MODES) * rows.astype(f32)
    damping = 1.0 + viscous_step * wave * wave
    for q in range(2):
        column = jnp.sum(jnp.where(diagonal, maps_ref[q : q + 1], 0.0), axis=1, keepdims=True)
        spread = (column == across).astype(f32)
        spreader_ref[q] = spread.astype(bf16)
        chooser_ref[q] = (maps_ref[2 + q : 3 + q] == along).astype(f32).astype(bf16)
        lane_chooser_ref[q] = (maps_ref[4 + q : 5 + q] == along).astype(f32).astype(bf16)
        first = jnp.sum(spread[0:TRACE], axis=0, keepdims=True)
        second = jnp.sum(spread[TRACE : 2 * TRACE], axis=0, keepdims=True)
        first = first * lower if q == 0 else first
        second = second * upper if q == 1 else second
        multiplicity = 1.0 + first + second
        weight_ref[q] = relaxation / (multiplicity * multiplicity)
        mass = jnp.concatenate([mass_ref[4 * q + i : 4 * q + i + 1] for i in range(4)], axis=1)
        row_mass_ref[q] = mass
        damped_ref[q] = damping * mass
    share = lax.rem(1024 - 64 * mode, 1024)
    first_half = lanes((2, 128)) < 64
    for start, ref in ((0, main_ref), (2, cross_ref)):
        part = pltpu.roll(ref[...], share, 1)[:, :128]
        metric_ref[start : start + 2] = jnp.where(first_half, part, pltpu.roll(part, 64, 1))
    slopes_out[...] = slopes_ref[...]
    basis_out[...] = basis_ref[...]
    slope_out[...] = slope_ref[...]
    forward_out[...] = forward_ref[...]


def advection_kernel(seen_ref, metric_ref, slopes_ref, basis_ref, slope_ref, forward_ref, send_ref):
    first_half = lanes((KZ, 128)) < 64
    field01 = seen_ref[:, 0].reshape(KZ, 128)
    field2 = seen_ref[:, 1].reshape(KZ, 128)
    fields = jnp.concatenate([field01, field2], axis=0)
    slopes = both(fields, slopes_ref)
    xi, eta = slopes[:, :128], slopes[:, 128:]
    grad_x = metric_ref[0:1] * xi + metric_ref[2:3] * eta
    grad_y = metric_ref[3:4] * xi + metric_ref[1:2] * eta
    other01 = pltpu.roll(field01, 64, 1)
    speed_u = jnp.where(first_half, field01, other01)
    speed_v = jnp.where(first_half, other01, field01)
    speed_w = jnp.where(first_half, field2, pltpu.roll(field2, 64, 1))

    def right(value):
        high, low = split(value)
        high = high.astype(bf16)
        return jnp.concatenate([high, high, low.astype(bf16)], axis=0)

    def physical(table_ref, value):
        return dot(table_ref[...], right(value))

    speeds = [physical(basis_ref, value) for value in (speed_u, speed_v, speed_w)]
    for part in range(2):
        keep = slice(KZ * part, KZ * (part + 1))
        advection = (
            speeds[0] * physical(basis_ref, grad_x[keep])
            + speeds[1] * physical(basis_ref, grad_y[keep])
            + speeds[2] * physical(slope_ref, fields[keep])
        )
        send_ref[:, part] = dot(forward_ref[...], right(advection)).reshape(16, 8, 128)


def table_kernel(
    precond_ref, stiffness_ref, chooser_ref, lane_chooser_ref, spreader_ref,
    inverse_ref, stiff_ref, column_ref, corner_ref, message_ref, reach_ref,
):
    k = pl.program_id(0)
    width = stiff_ref.shape[2]
    block = pl.ds(pl.multiple_of(TRACE * k, TRACE), TRACE)
    mine = lanes((width, 128)) // TRACE == k

    @pl.when(k == 0)
    def _():
        for q in range(2):
            for part, value in enumerate(split(viscous_step * stiffness_ref[width * q : width * (q + 1)])):
                stiff_ref[q, part] = value.astype(bf16)
        reach_ref[...] = jnp.zeros_like(reach_ref)

    for q in range(2):
        parts = [value.astype(bf16) for value in split(precond_ref[0, width * q : width * (q + 1)].T)]
        spreader = spreader_ref[q, TRACE * q : TRACE * (q + 1)]
        lane_chooser = jnp.where(mine, lane_chooser_ref[q].astype(f32), 0.0).astype(bf16)
        corner = 0.0
        for part in range(2):
            inverse_ref[k, q, part] = parts[part]
            column = dot(spreader, parts[part]).astype(bf16)
            column_ref[q, part, block] = column
            corner = corner + dot(column, chooser_ref[q])
            reach = dot(parts[part], lane_chooser)
            reach_ref[q, part] = (reach_ref[q, part].astype(f32) + reach).astype(bf16)
        message_ref[q, block] = corner
        for part, value in enumerate(split(corner)):
            corner_ref[q, part, block] = value.astype(bf16)


def link_kernel(lower_ref, upper_ref, gate_ref, link_ref):
    for q, ref in enumerate((lower_ref, upper_ref)):
        for part, value in enumerate(split(ref[32:160] * gate_ref[q : q + 1])):
            link_ref[q, part] = value.astype(bf16)


def send_traces(residual, reach_ref, chooser_ref, spreader_ref, outs):
    gained_ref, trace_ref, up_ref, down_ref = outs
    lane = lanes((32, 128))
    trace = [pick(residual[q], chooser_ref[q]) for q in range(2)]
    inner = [
        jnp.where((lane >= TRACE) & (lane < 2 * TRACE), trace[1], 0.0),
        jnp.where(lane < TRACE, trace[0], 0.0),
    ]
    for q in range(2):
        gained = residual[q] + scatter(inner[q], spreader_ref[q])
        gained_ref[q] = gained
        trace_ref[q] = trace[q]
        reached = unblocked(both(gained, reach_ref.at[q]), 96 if q == 0 else 64)
        (down_ref, up_ref)[q][0:32] = trace[q] + reached


def precondition_kernel(gained_ref, inverse_ref, chooser_ref, part_ref, trace_ref):
    def one_mode(k, carry):
        rows = pl.ds(pl.multiple_of(SLOT * k, SLOT), SLOT)
        for q in range(2):
            part_ref[q, rows] = both(gained_ref[q, rows], inverse_ref.at[k, q])
        return carry

    lax.fori_loop(0, 4, one_mode, 0)
    for q in range(2):
        trace_ref[q] = pick(part_ref[q], chooser_ref[q])


def first_kernel(
    seen_ref, state_ref, mass_ref, reach_ref, chooser_ref, spreader_ref, *refs
):
    refs = list(refs)
    corners_ref = refs.pop(0) if len(refs) > 5 else None
    local_ref, gained_ref, trace_ref, up_ref, down_ref = refs
    first_half = lanes((8, 128)) < 64
    local_ref[...] = jnp.zeros_like(local_ref)
    per_patch = local_ref.shape[2] // 128
    for t in range(8):
        a0, b0 = seen_ref[2 * t, 0], seen_ref[2 * t + 1, 0]
        a1, b1 = seen_ref[2 * t, 1], seen_ref[2 * t + 1, 1]
        fields = [
            jnp.where(first_half, a0, pltpu.roll(b0, 64, 1)),
            jnp.where(first_half, pltpu.roll(a0, 64, 1), b0),
            jnp.where(first_half, a1, pltpu.roll(b1, 64, 1)),
        ]
        where = slice(128 * (t % per_patch), 128 * (t % per_patch + 1))
        for k in range(4):
            for c in range(3):
                local_ref[t // per_patch, SLOT * k + 2 * c : SLOT * k + 2 * c + 2, where] = fields[c][
                    2 * k : 2 * k + 2
                ]
    local = [mass_ref[q] * (state_ref[q] - time_step * local_ref[q]) for q in range(2)]
    for q in range(2):
        local_ref[q] = local[q]
    send_traces(local, reach_ref, chooser_ref, spreader_ref, (gained_ref, trace_ref, up_ref, down_ref))
    if corners_ref is not None:
        down_ref[32:160] = corners_ref[0]
        up_ref[32:160] = corners_ref[1]


def update(
    lower_ref, upper_ref, part_ref, part_trace_ref, trace_ref, gate_ref, weight_ref, column_ref,
    corner_ref, link_ref, spreader_ref,
):
    lane = lanes((32, 128))
    low = lane < TRACE
    high = (lane >= TRACE) & (lane < 2 * TRACE)
    lower = jnp.where(gate_ref[0:1] > 0.0, lower_ref[0:32], 0.0)
    upper = jnp.where(gate_ref[1:2] > 0.0, upper_ref[0:32], 0.0)
    inflow = [blocked(lower, 0), blocked(upper, TRACE)]
    linked = [both(blocked(trace_ref[q], TRACE * (1 - q)), link_ref.at[q]) for q in range(2)]
    inner = [part_trace_ref[q] + both(inflow[q], corner_ref.at[q]) for q in range(2)]
    gains = [
        jnp.where(low, pltpu.roll(lower, 64, 1) + linked[0], jnp.where(high, inner[1], 0.0)),
        jnp.where(high, pltpu.roll(upper, 64, 1) + linked[1], jnp.where(low, inner[0], 0.0)),
    ]
    return [
        weight_ref[q]
        * (part_ref[q] + both(inflow[q], column_ref.at[q]) + scatter(gains[q], spreader_ref[q]))
        for q in range(2)
    ]


def sweep_kernel(fresh, *refs):
    refs = list(refs)
    iterate_ref = None if fresh else refs.pop(0)
    received, refs = refs[:11], refs[11:]
    (
        local_ref, chooser_ref, damped_ref, stiff_ref, reach_ref,
        next_ref, gained_ref, trace_ref, up_ref, down_ref,
    ) = refs
    spreader_ref = received[-1]
    step = update(*received)
    residual = []
    for q in range(2):
        iterate = step[q] if fresh else iterate_ref[q] + step[q]
        next_ref[q] = iterate
        residual.append(local_ref[q] - both(iterate, stiff_ref.at[q]) - damped_ref[q] * iterate)
    send_traces(residual, reach_ref, chooser_ref, spreader_ref, (gained_ref, trace_ref, up_ref, down_ref))


def last_kernel(final, iterate_ref, *refs):
    received, outs = refs[:11], refs[11:]
    step = update(*received)
    state = [iterate_ref[q] + step[q] for q in range(2)]
    field_ref = outs[0] if final else outs[2]
    width = state[0].shape[1]
    for q in range(2):
        for k in range(4):
            for c in range(3):
                field_ref[c, 2 * k : 2 * k + 2, width * q : width * (q + 1)] = state[q][
                    SLOT * k + 2 * c : SLOT * k + 2 * c + 2
                ]
    if not final:
        send_ref, state_ref = outs[0], outs[1]
        for q in range(2):
            state_ref[q] = state[q]
        pack_points([field_ref[c] for c in range(3)], send_ref)


VMEM = pl.BlockSpec(memory_space=pltpu.VMEM)
SCOPED = 24 << 20


def call(kernel, outs, *args, scratch=(), name=None, flops=0):
    single = not isinstance(outs, (list, tuple))
    shapes = [outs] if single else list(outs)
    cost = pl.CostEstimate(flops=flops, bytes_accessed=0, transcendentals=0) if flops else None
    return pl.pallas_call(
        kernel,
        out_shape=shapes[0] if single else shapes,
        in_specs=[VMEM] * len(args),
        out_specs=VMEM if single else [VMEM] * len(shapes),
        scratch_shapes=list(scratch),
        name=name,
        cost_estimate=cost,
        compiler_params=pltpu.CompilerParams(vmem_limit_bytes=SCOPED),
    )(*args)


def in_hbm(value):
    return pltpu.with_memory_space_constraint(value, pltpu.HBM)


def shape(*dims, dtype=f32):
    return jax.ShapeDtypeStruct(dims, dtype)


def on_device(velocity, metric_main, metric_cross, stiffness, mass, precond, trace_map):
    points = velocity.shape[2]
    width = stiffness.shape[1]
    patches = trace_map.shape[0]
    mode_count = lax.axis_size("mode")
    elem_count = lax.axis_size("elem")
    mode_index = lax.axis_index("mode")
    elem_index = lax.axis_index("elem")
    share = points // mode_count

    packed = shape(16, 2, 8, 128)
    solver = shape(2, 32, width)
    trace_pair = shape(2, 32, 128)
    message = shape(32, 128)
    send, state = call(start_kernel, [packed, solver], in_hbm(velocity), name="start")

    lower_map, upper_map = [trace_map[:, side].astype(f32) for side in range(2)]
    nowhere = jnp.full_like(lower_map, -1.0)
    maps = jnp.concatenate(
        [
            jnp.concatenate([lower_map, upper_map, lower_map, upper_map], axis=1),
            jnp.concatenate([upper_map, lower_map, nowhere, nowhere], axis=1),
            jnp.tile(jnp.stack([lower_map[0], upper_map[1]]), (1, 4)),
        ]
    )
    index = jnp.stack([mode_index, elem_index, jnp.full_like(elem_index, elem_count - 1)])
    tables = [jnp.asarray(table) for table in (slope_weights(), *spanwise_tables())]
    small = [
        shape(patches, 128, width, dtype=bf16),
        shape(patches, width, 128, dtype=bf16),
        shape(patches, width, 128, dtype=bf16),
        shape(patches, 1, width),
        shape(2, 128),
        shape(patches, 1, width),
        shape(patches, 32, width),
        shape(4, 128),
    ] + [shape(*table.shape, dtype=bf16) for table in tables]
    (
        spreader, chooser, lane_chooser, weight, gate, patch_mass, damped, metric,
        slopes, basis, slope, forward,
    ) = pl.pallas_call(
        setup_kernel,
        out_shape=small,
        in_specs=[pl.BlockSpec(memory_space=pltpu.SMEM)] + [VMEM] * 8,
        out_specs=[VMEM] * 12,
        name="setup",
        compiler_params=pltpu.CompilerParams(vmem_limit_bytes=SCOPED),
    )(index, maps, *[in_hbm(value) for value in (mass.reshape(8, -1), metric_main, metric_cross, *tables)])

    up = [(i, (i + 1) % elem_count) for i in range(elem_count)]
    down = [((i + 1) % elem_count, i) for i in range(elem_count)]

    def neighbours(upward, downward):
        return lax.ppermute(upward, "elem", up), lax.ppermute(downward, "elem", down)

    def transpose(value):
        return lax.all_to_all(value, "mode", split_axis=0, concat_axis=0, tiled=True)

    def precondition(gained):
        return call(
            precondition_kernel, [solver, trace_pair], gained, inverse, chooser,
            name="precondition", flops=8 * 4 * 2 * 16 * width * width,
        )

    for time_level in range(STEPS):
        send = call(
            advection_kernel, packed, transpose(send), metric, slopes, basis, slope, forward, name="advection"
        )
        seen = transpose(send)
        opening = time_level == 0
        if opening:
            seen, precond = lax.optimization_barrier((seen, precond))
            inverse, stiff, column, corner, corners, reach = pl.pallas_call(
                table_kernel,
                grid=(4,),
                out_shape=[
                    shape(4, 2, 2, width, width, dtype=bf16),
                    shape(2, 2, width, width, dtype=bf16),
                    shape(2, 2, 128, width, dtype=bf16),
                    shape(2, 2, 128, 128, dtype=bf16),
                    shape(2, 128, 128),
                    shape(2, 2, width, 128, dtype=bf16),
                ],
                in_specs=[pl.BlockSpec((1, patches * width, width), lambda k: (k, 0, 0))] + [VMEM] * 4,
                out_specs=[VMEM] * 6,
                name="tables",
                compiler_params=pltpu.CompilerParams(vmem_limit_bytes=SCOPED),
            )(in_hbm(precond), in_hbm(stiffness), chooser, lane_chooser, spreader)
        sent = shape(160, 128) if opening else message
        local, gained, trace, upward, downward = call(
            first_kernel, [solver, solver, trace_pair, sent, sent],
            seen, state, patch_mass, reach, chooser, spreader,
            *((corners,) if opening else ()), name="first",
        )
        iterate = ()
        for sweep_number in range(ITERS):
            lower, upper = neighbours(upward, downward)
            part, part_trace = precondition(gained)
            if opening and sweep_number == 0:
                link = call(
                    link_kernel, shape(2, 2, 128, 128, dtype=bf16), lower, upper, gate, name="links"
                )
            received = (lower, upper, part, part_trace, trace, gate, weight, column, corner, link, spreader)
            if sweep_number < ITERS - 1:
                iterate, gained, trace, upward, downward = call(
                    functools.partial(sweep_kernel, sweep_number == 0),
                    [solver, solver, trace_pair, message, message],
                    *iterate, *received, local, chooser, damped, stiff, reach, name="sweep",
                )
                iterate = (iterate,)
            elif time_level < STEPS - 1:
                send, state = call(
                    functools.partial(last_kernel, False), [packed, solver], *iterate, *received,
                    scratch=[pltpu.VMEM((3, 8, points), f32)], name="last",
                )
            else:
                state = call(
                    functools.partial(last_kernel, True), shape(3, 8, points), *iterate, *received, name="final"
                )
    return state


def solution(mesh):
    return jax.shard_map(
        on_device,
        mesh=mesh,
        in_specs=(
            P(None, "mode", "elem"),
            P(None, "elem"),
            P(None, "elem"),
            P("elem", None),
            P("elem"),
            P("mode", "elem", None),
            P("elem", None, None),
        ),
        out_specs=P(None, "mode", "elem"),
        check_vma=False,
    )
```

```python
import functools
import math

import jax
import jax.numpy as jnp
import numpy as np
from jax import lax
from jax.experimental import pallas as pl
from jax.experimental.pallas import tpu as pltpu
from jax.sharding import PartitionSpec as P

MODES = 64
KZ = 128
NZ = 256
STEPS = 4
ITERS = 4
TRACE = 32
SLOT = 8

viscous_step = 0.5
time_step = 0.02
relaxation = 0.8

f32 = jnp.float32
bf16 = jnp.bfloat16


def chebyshev_matrix():
    node_points = np.cos(np.pi * np.arange(8) / 7.0)
    weights = np.where((np.arange(8) == 0) | (np.arange(8) == 7), 2.0, 1.0)
    parity = np.where((np.arange(8)[:, None] + np.arange(8)[None, :]) % 2 == 0, 1.0, -1.0)
    identity = np.eye(8)
    spacing = node_points[:, None] - node_points[None, :] + identity
    off_diagonal = weights[:, None] / weights[None, :] * parity / spacing * (1.0 - identity)
    return off_diagonal - identity * off_diagonal.sum(axis=1)[:, None]


def halves(table):
    table = np.asarray(table, np.float32)
    high = table.astype(bf16)
    low = (table - high.astype(np.float32)).astype(bf16)
    return high, low


def spanwise_tables():
    rows = np.arange(KZ)
    wavenumber = rows // 2
    product = (np.arange(NZ)[:, None] * wavenumber[None, :]) % NZ
    phase = 2.0 * math.pi / NZ * product
    sine = (rows % 2 == 1)[None, :]
    rate = 4.0 * wavenumber / MODES
    basis = np.where(sine, np.sin(phase), np.cos(phase))
    slope = np.where(sine, rate * np.cos(phase), -rate * np.sin(phase))
    forward = basis.T * np.where(rows == 0, 1.0 / NZ, 2.0 / NZ)[:, None]

    def left(table):
        high, low = halves(table)
        return np.concatenate([high, low, high], axis=1)

    return left(basis), left(slope), left(forward)


def slope_weights():
    chebyshev = chebyshev_matrix()
    along_xi = np.kron(np.eye(8), chebyshev.T)
    along_eta = np.kron(chebyshev.T, np.eye(8))
    both = np.concatenate([np.kron(np.eye(2), along_xi), np.kron(np.eye(2), along_eta)], axis=1)
    high, low = halves(both)
    return np.stack([high, low])


def split(value):
    high = value.astype(bf16).astype(f32)
    return high, value - high


def stacked(value):
    return jnp.concatenate(split(value), axis=0).astype(bf16)


def folded(value):
    half = value.shape[0] // 2
    return value[:half] + value[half:]


def dot(a, b):
    return jnp.dot(a, b, preferred_element_type=f32)


def lanes(shape):
    return lax.broadcasted_iota(jnp.int32, shape, len(shape) - 1)


def pick(value, chooser):
    return folded(dot(stacked(value), chooser))


def scatter(trace, spreader):
    high, low = split(trace)
    return dot((high + pltpu.roll(low, 64, 1)).astype(bf16), spreader)


def both(value, table_ref):
    rows = stacked(value)
    return folded(dot(rows, table_ref[0]) + dot(rows, table_ref[1]))


def mode_rows(value, k):
    return value[SLOT * k : SLOT * (k + 1)]


def turned(value, start, stop):
    parts = []
    for k in range(4):
        by = (stop(k) - start(k)) % 128
        rows = mode_rows(value, k)
        parts.append(pltpu.roll(rows, by, 1) if by else rows)
    return jnp.concatenate(parts, axis=0)


def own_block():
    return lanes((32, 128)) // TRACE == lax.broadcasted_iota(jnp.int32, (32, 128), 0) // SLOT


def blocked(value, lane):
    return jnp.where(own_block(), turned(value, lambda k: lane, lambda k: TRACE * k), 0.0)


def unblocked(value, lane):
    return turned(jnp.where(own_block(), value, 0.0), lambda k: TRACE * k, lambda k: lane)


def pack_points(fields, send_ref):
    first_half = lanes((8, 128)) < 64
    for t in range(8):
        c0, c1, c2 = [fields[c][:, 128 * t : 128 * (t + 1)] for c in range(3)]
        send_ref[2 * t, 0] = jnp.where(first_half, c0, pltpu.roll(c1, 64, 1))
        send_ref[2 * t + 1, 0] = jnp.where(first_half, pltpu.roll(c0, 64, 1), c1)
        send_ref[2 * t, 1] = jnp.where(first_half, c2, 0.0)
        send_ref[2 * t + 1, 1] = jnp.where(first_half, pltpu.roll(c2, 64, 1), 0.0)


def start_kernel(velocity_ref, send_ref, state_ref):
    pack_points([velocity_ref[c] for c in range(3)], send_ref)
    state_ref[...] = jnp.zeros_like(state_ref)
    width = state_ref.shape[2]
    for q in range(state_ref.shape[0]):
        for k in range(4):
            for c in range(3):
                state_ref[q, SLOT * k + 2 * c : SLOT * k + 2 * c + 2, :] = velocity_ref[
                    c, 2 * k : 2 * k + 2, width * q : width * (q + 1)
                ]


def setup_kernel(
    index_ref, maps_ref, mass_ref, main_ref, cross_ref, slopes_ref, basis_ref, slope_ref, forward_ref,
    spreader_ref, chooser_ref, lane_chooser_ref, weight_ref, gate_ref, row_mass_ref, damped_ref, metric_ref,
    slopes_out, basis_out, slope_out, forward_out,
):
    mode, elem, last = index_ref[0], index_ref[1], index_ref[2]
    width = spreader_ref.shape[2]
    lower = jnp.where(elem > 0, 1.0, 0.0)
    upper = jnp.where(elem < last, 1.0, 0.0)
    gate_ref[0:1] = jnp.full((1, 128), lower, f32)
    gate_ref[1:2] = jnp.full((1, 128), upper, f32)
    diagonal = lax.broadcasted_iota(jnp.int32, (128, 128), 0) == lanes((128, 128))
    across = lanes((128, width)).astype(f32)
    along = lax.broadcasted_iota(jnp.int32, (width, 128), 0).astype(f32)
    rows = lax.broadcasted_iota(jnp.int32, (32, width), 0) // SLOT + 4 * mode
    wave = (4.0 / MODES) * rows.astype(f32)
    damping = 1.0 + viscous_step * wave * wave
    for q in range(2):
        column = jnp.sum(jnp.where(diagonal, maps_ref[q : q + 1], 0.0), axis=1, keepdims=True)
        spread = (column == across).astype(f32)
        spreader_ref[q] = spread.astype(bf16)
        chooser_ref[q] = (maps_ref[2 + q : 3 + q] == along).astype(f32).astype(bf16)
        lane_chooser_ref[q] = (maps_ref[4 + q : 5 + q] == along).astype(f32).astype(bf16)
        first = jnp.sum(spread[0:TRACE], axis=0, keepdims=True)
        second = jnp.sum(spread[TRACE : 2 * TRACE], axis=0, keepdims=True)
        first = first * lower if q == 0 else first
        second = second * upper if q == 1 else second
        multiplicity = 1.0 + first + second
        weight_ref[q] = relaxation / (multiplicity * multiplicity)
        mass = jnp.concatenate([mass_ref[4 * q + i : 4 * q + i + 1] for i in range(4)], axis=1)
        row_mass_ref[q] = mass
        damped_ref[q] = damping * mass
    share = lax.rem(1024 - 64 * mode, 1024)
    first_half = lanes((2, 128)) < 64
    for start, ref in ((0, main_ref), (2, cross_ref)):
        part = pltpu.roll(ref[...], share, 1)[:, :128]
        metric_ref[start : start + 2] = jnp.where(first_half, part, pltpu.roll(part, 64, 1))
    slopes_out[...] = slopes_ref[...]
    basis_out[...] = basis_ref[...]
    slope_out[...] = slope_ref[...]
    forward_out[...] = forward_ref[...]


def advection_kernel(seen_ref, metric_ref, slopes_ref, basis_ref, slope_ref, forward_ref, send_ref):
    first_half = lanes((KZ, 128)) < 64
    field01 = seen_ref[:, 0].reshape(KZ, 128)
    field2 = seen_ref[:, 1].reshape(KZ, 128)
    fields = jnp.concatenate([field01, field2], axis=0)
    slopes = both(fields, slopes_ref)
    xi, eta = slopes[:, :128], slopes[:, 128:]
    grad_x = metric_ref[0:1] * xi + metric_ref[2:3] * eta
    grad_y = metric_ref[3:4] * xi + metric_ref[1:2] * eta
    other01 = pltpu.roll(field01, 64, 1)
    speed_u = jnp.where(first_half, field01, other01)
    speed_v = jnp.where(first_half, other01, field01)
    speed_w = jnp.where(first_half, field2, pltpu.roll(field2, 64, 1))

    def right(value):
        high, low = split(value)
        high = high.astype(bf16)
        return jnp.concatenate([high, high, low.astype(bf16)], axis=0)

    def physical(table_ref, value):
        return dot(table_ref[...], right(value))

    speeds = [physical(basis_ref, value) for value in (speed_u, speed_v, speed_w)]
    for part in range(2):
        keep = slice(KZ * part, KZ * (part + 1))
        advection = (
            speeds[0] * physical(basis_ref, grad_x[keep])
            + speeds[1] * physical(basis_ref, grad_y[keep])
            + speeds[2] * physical(slope_ref, fields[keep])
        )
        send_ref[:, part] = dot(forward_ref[...], right(advection)).reshape(16, 8, 128)


def table_kernel(
    precond_ref, stiffness_ref, chooser_ref, lane_chooser_ref, spreader_ref,
    inverse_ref, stiff_ref, column_ref, corner_ref, message_ref, reach_ref,
):
    k = pl.program_id(0)
    width = stiff_ref.shape[2]
    block = pl.ds(pl.multiple_of(TRACE * k, TRACE), TRACE)
    mine = lanes((width, 128)) // TRACE == k

    @pl.when(k == 0)
    def _():
        for q in range(2):
            for part, value in enumerate(split(viscous_step * stiffness_ref[width * q : width * (q + 1)])):
                stiff_ref[q, part] = value.astype(bf16)
        reach_ref[...] = jnp.zeros_like(reach_ref)

    for q in range(2):
        parts = [value.astype(bf16) for value in split(precond_ref[0, width * q : width * (q + 1)].T)]
        spreader = spreader_ref[q, TRACE * q : TRACE * (q + 1)]
        lane_chooser = jnp.where(mine, lane_chooser_ref[q].astype(f32), 0.0).astype(bf16)
        corner = 0.0
        for part in range(2):
            inverse_ref[k, q, part] = parts[part]
            column = dot(spreader, parts[part]).astype(bf16)
            column_ref[q, part, block] = column
            corner = corner + dot(column, chooser_ref[q])
            reach = dot(parts[part], lane_chooser)
            reach_ref[q, part] = (reach_ref[q, part].astype(f32) + reach).astype(bf16)
        message_ref[q, block] = corner
        for part, value in enumerate(split(corner)):
            corner_ref[q, part, block] = value.astype(bf16)


def link_kernel(lower_ref, upper_ref, gate_ref, link_ref):
    for q, ref in enumerate((lower_ref, upper_ref)):
        for part, value in enumerate(split(ref[32:160] * gate_ref[q : q + 1])):
            link_ref[q, part] = value.astype(bf16)


def send_traces(residual, reach_ref, chooser_ref, spreader_ref, outs):
    gained_ref, trace_ref, up_ref, down_ref = outs
    lane = lanes((32, 128))
    trace = [pick(residual[q], chooser_ref[q]) for q in range(2)]
    inner = [
        jnp.where((lane >= TRACE) & (lane < 2 * TRACE), trace[1], 0.0),
        jnp.where(lane < TRACE, trace[0], 0.0),
    ]
    for q in range(2):
        gained = residual[q] + scatter(inner[q], spreader_ref[q])
        gained_ref[q] = gained
        trace_ref[q] = trace[q]
        reached = unblocked(both(gained, reach_ref.at[q]), 96 if q == 0 else 64)
        (down_ref, up_ref)[q][0:32] = trace[q] + reached


def precondition_kernel(gained_ref, inverse_ref, chooser_ref, part_ref, trace_ref):
    def one_mode(k, carry):
        rows = pl.ds(pl.multiple_of(SLOT * k, SLOT), SLOT)
        for q in range(2):
            part_ref[q, rows] = both(gained_ref[q, rows], inverse_ref.at[k, q])
        return carry

    lax.fori_loop(0, 4, one_mode, 0)
    for q in range(2):
        trace_ref[q] = pick(part_ref[q], chooser_ref[q])


def first_kernel(
    seen_ref, state_ref, mass_ref, reach_ref, chooser_ref, spreader_ref, *refs
):
    refs = list(refs)
    corners_ref = refs.pop(0) if len(refs) > 5 else None
    local_ref, gained_ref, trace_ref, up_ref, down_ref = refs
    first_half = lanes((8, 128)) < 64
    local_ref[...] = jnp.zeros_like(local_ref)
    per_patch = local_ref.shape[2] // 128
    for t in range(8):
        a0, b0 = seen_ref[2 * t, 0], seen_ref[2 * t + 1, 0]
        a1, b1 = seen_ref[2 * t, 1], seen_ref[2 * t + 1, 1]
        fields = [
            jnp.where(first_half, a0, pltpu.roll(b0, 64, 1)),
            jnp.where(first_half, pltpu.roll(a0, 64, 1), b0),
            jnp.where(first_half, a1, pltpu.roll(b1, 64, 1)),
        ]
        where = slice(128 * (t % per_patch), 128 * (t % per_patch + 1))
        for k in range(4):
            for c in range(3):
                local_ref[t // per_patch, SLOT * k + 2 * c : SLOT * k + 2 * c + 2, where] = fields[c][
                    2 * k : 2 * k + 2
                ]
    local = [mass_ref[q] * (state_ref[q] - time_step * local_ref[q]) for q in range(2)]
    for q in range(2):
        local_ref[q] = local[q]
    send_traces(local, reach_ref, chooser_ref, spreader_ref, (gained_ref, trace_ref, up_ref, down_ref))
    if corners_ref is not None:
        down_ref[32:160] = corners_ref[0]
        up_ref[32:160] = corners_ref[1]


def update(
    lower_ref, upper_ref, part_ref, part_trace_ref, trace_ref, gate_ref, weight_ref, column_ref,
    corner_ref, link_ref, spreader_ref,
):
    lane = lanes((32, 128))
    low = lane < TRACE
    high = (lane >= TRACE) & (lane < 2 * TRACE)
    lower = jnp.where(gate_ref[0:1] > 0.0, lower_ref[0:32], 0.0)
    upper = jnp.where(gate_ref[1:2] > 0.0, upper_ref[0:32], 0.0)
    inflow = [blocked(lower, 0), blocked(upper, TRACE)]
    linked = [both(blocked(trace_ref[q], TRACE * (1 - q)), link_ref.at[q]) for q in range(2)]
    inner = [part_trace_ref[q] + both(inflow[q], corner_ref.at[q]) for q in range(2)]
    gains = [
        jnp.where(low, pltpu.roll(lower, 64, 1) + linked[0], jnp.where(high, inner[1], 0.0)),
        jnp.where(high, pltpu.roll(upper, 64, 1) + linked[1], jnp.where(low, inner[0], 0.0)),
    ]
    return [
        weight_ref[q]
        * (part_ref[q] + both(inflow[q], column_ref.at[q]) + scatter(gains[q], spreader_ref[q]))
        for q in range(2)
    ]


def sweep_kernel(fresh, *refs):
    refs = list(refs)
    iterate_ref = None if fresh else refs.pop(0)
    received, refs = refs[:11], refs[11:]
    (
        local_ref, chooser_ref, damped_ref, stiff_ref, reach_ref,
        next_ref, gained_ref, trace_ref, up_ref, down_ref,
    ) = refs
    spreader_ref = received[-1]
    step = update(*received)
    residual = []
    for q in range(2):
        iterate = step[q] if fresh else iterate_ref[q] + step[q]
        next_ref[q] = iterate
        residual.append(local_ref[q] - both(iterate, stiff_ref.at[q]) - damped_ref[q] * iterate)
    send_traces(residual, reach_ref, chooser_ref, spreader_ref, (gained_ref, trace_ref, up_ref, down_ref))


def last_kernel(level_ref, iterate_ref, *refs):
    received, (level_out, send_ref, state_ref, field_ref) = refs[:11], refs[11:]
    level_out[...] = level_ref[...] + 1
    step = update(*received)
    state = [iterate_ref[q] + step[q] for q in range(2)]
    width = state[0].shape[1]
    for q in range(2):
        state_ref[q] = state[q]
        for k in range(4):
            for c in range(3):
                field_ref[c, 2 * k : 2 * k + 2, width * q : width * (q + 1)] = state[q][
                    SLOT * k + 2 * c : SLOT * k + 2 * c + 2
                ]
    pack_points([field_ref[c] for c in range(3)], send_ref)


VMEM = pl.BlockSpec(memory_space=pltpu.VMEM)
SCOPED = 24 << 20


def call(kernel, outs, *args, scratch=(), name=None, flops=0):
    single = not isinstance(outs, (list, tuple))
    shapes = [outs] if single else list(outs)
    cost = pl.CostEstimate(flops=flops, bytes_accessed=0, transcendentals=0) if flops else None
    return pl.pallas_call(
        kernel,
        out_shape=shapes[0] if single else shapes,
        in_specs=[VMEM] * len(args),
        out_specs=VMEM if single else [VMEM] * len(shapes),
        scratch_shapes=list(scratch),
        name=name,
        cost_estimate=cost,
        compiler_params=pltpu.CompilerParams(vmem_limit_bytes=SCOPED),
    )(*args)


def in_hbm(value):
    return pltpu.with_memory_space_constraint(value, pltpu.HBM)


def shape(*dims, dtype=f32):
    return jax.ShapeDtypeStruct(dims, dtype)


def on_device(velocity, metric_main, metric_cross, stiffness, mass, precond, trace_map):
    points = velocity.shape[2]
    width = stiffness.shape[1]
    patches = trace_map.shape[0]
    mode_count = lax.axis_size("mode")
    elem_count = lax.axis_size("elem")
    mode_index = lax.axis_index("mode")
    elem_index = lax.axis_index("elem")
    share = points // mode_count

    packed = shape(16, 2, 8, 128)
    solver = shape(2, 32, width)
    trace_pair = shape(2, 32, 128)
    message = shape(32, 128)
    send, state = call(start_kernel, [packed, solver], in_hbm(velocity), name="start")

    lower_map, upper_map = [trace_map[:, side].astype(f32) for side in range(2)]
    nowhere = jnp.full_like(lower_map, -1.0)
    maps = jnp.concatenate(
        [
            jnp.concatenate([lower_map, upper_map, lower_map, upper_map], axis=1),
            jnp.concatenate([upper_map, lower_map, nowhere, nowhere], axis=1),
            jnp.tile(jnp.stack([lower_map[0], upper_map[1]]), (1, 4)),
        ]
    )
    index = jnp.stack([mode_index, elem_index, jnp.full_like(elem_index, elem_count - 1)])
    tables = [jnp.asarray(table) for table in (slope_weights(), *spanwise_tables())]
    small = [
        shape(patches, 128, width, dtype=bf16),
        shape(patches, width, 128, dtype=bf16),
        shape(patches, width, 128, dtype=bf16),
        shape(patches, 1, width),
        shape(2, 128),
        shape(patches, 1, width),
        shape(patches, 32, width),
        shape(4, 128),
    ] + [shape(*table.shape, dtype=bf16) for table in tables]
    (
        spreader, chooser, lane_chooser, weight, gate, patch_mass, damped, metric,
        slopes, basis, slope, forward,
    ) = pl.pallas_call(
        setup_kernel,
        out_shape=small,
        in_specs=[pl.BlockSpec(memory_space=pltpu.SMEM)] + [VMEM] * 8,
        out_specs=[VMEM] * 12,
        name="setup",
        compiler_params=pltpu.CompilerParams(vmem_limit_bytes=SCOPED),
    )(index, maps, *[in_hbm(value) for value in (mass.reshape(8, -1), metric_main, metric_cross, *tables)])

    up = [(i, (i + 1) % elem_count) for i in range(elem_count)]
    down = [((i + 1) % elem_count, i) for i in range(elem_count)]

    def neighbours(upward, downward):
        return lax.ppermute(upward, "elem", up), lax.ppermute(downward, "elem", down)

    def transpose(value):
        return lax.all_to_all(value, "mode", split_axis=0, concat_axis=0, tiled=True)

    def precondition(gained):
        return call(
            precondition_kernel, [solver, trace_pair], gained, inverse, chooser,
            name="precondition", flops=8 * 4 * 2 * 16 * width * width,
        )

    def advect(send):
        seen = transpose(send)
        return transpose(
            call(advection_kernel, packed, seen, metric, slopes, basis, slope, forward, name="advection")
        )

    def begin(seen, state, corners):
        sent = shape(160, 128) if corners else message
        return call(
            first_kernel, [solver, solver, trace_pair, sent, sent],
            seen, state, patch_mass, reach, chooser, spreader, *corners, name="first",
        )

    def solve(level, local, gained, trace, upward, downward, link):
        iterate = ()
        for sweep_number in range(ITERS):
            lower, upper = neighbours(upward, downward)
            part, part_trace = precondition(gained)
            if link is None:
                link = call(
                    link_kernel, shape(2, 2, 128, 128, dtype=bf16), lower, upper, gate, name="links"
                )
            received = (lower, upper, part, part_trace, trace, gate, weight, column, corner, link, spreader)
            if sweep_number < ITERS - 1:
                iterate, gained, trace, upward, downward = call(
                    functools.partial(sweep_kernel, sweep_number == 0),
                    [solver, solver, trace_pair, message, message],
                    *iterate, *received, local, chooser, damped, stiff, reach, name="sweep",
                )
                iterate = (iterate,)
        args = (level, *iterate, *received)
        level, send, state, field = pl.pallas_call(
            last_kernel,
            out_shape=[shape(8, 128, dtype=jnp.int32), packed, solver, shape(3, 8, points)],
            in_specs=[VMEM] * len(args),
            out_specs=[VMEM] * 4,
            input_output_aliases={0: 0},
            name="last",
            compiler_params=pltpu.CompilerParams(vmem_limit_bytes=SCOPED),
        )(*args)
        return level, send, state, field, link

    seen, precond = lax.optimization_barrier((advect(send), precond))
    inverse, stiff, column, corner, corners, reach = pl.pallas_call(
            table_kernel,
            grid=(4,),
            out_shape=[
                shape(4, 2, 2, width, width, dtype=bf16),
                shape(2, 2, width, width, dtype=bf16),
                shape(2, 2, 128, width, dtype=bf16),
                shape(2, 2, 128, 128, dtype=bf16),
                shape(2, 128, 128),
                shape(2, 2, width, 128, dtype=bf16),
            ],
            in_specs=[pl.BlockSpec((1, patches * width, width), lambda k: (k, 0, 0))] + [VMEM] * 4,
            out_specs=[VMEM] * 6,
            name="tables",
            compiler_params=pltpu.CompilerParams(vmem_limit_bytes=SCOPED),
        )(in_hbm(precond), in_hbm(stiffness), chooser, lane_chooser, spreader)
    start = jnp.zeros((8, 128), jnp.int32)
    level, send, state, field, link = solve(start, *begin(seen, state, (corners,)), None)

    def step(carried):
        level, send, state, _ = carried
        return solve(level, *begin(advect(send), state, ()), link)[:4]

    return lax.while_loop(lambda carried: carried[0][0, 0] < STEPS, step, (level, send, state, field))[3]


def solution(mesh):
    return jax.shard_map(
        on_device,
        mesh=mesh,
        in_specs=(
            P(None, "mode", "elem"),
            P(None, "elem"),
            P(None, "elem"),
            P("elem", None),
            P("elem"),
            P("mode", "elem", None),
            P("elem", None, None),
        ),
        out_specs=P(None, "mode", "elem"),
        check_vma=False,
    )
```

```python
import functools
import math

import jax
import jax.numpy as jnp
import numpy as np
from jax import lax
from jax.experimental import pallas as pl
from jax.experimental.pallas import tpu as pltpu
from jax.sharding import PartitionSpec as P

MODES = 64
KZ = 128
NZ = 256
STEPS = 4
ITERS = 4
TRACE = 32
SLOT = 8

viscous_step = 0.5
time_step = 0.02
relaxation = 0.8

f32 = jnp.float32
bf16 = jnp.bfloat16


def chebyshev_matrix():
    node_points = np.cos(np.pi * np.arange(8) / 7.0)
    weights = np.where((np.arange(8) == 0) | (np.arange(8) == 7), 2.0, 1.0)
    parity = np.where((np.arange(8)[:, None] + np.arange(8)[None, :]) % 2 == 0, 1.0, -1.0)
    identity = np.eye(8)
    spacing = node_points[:, None] - node_points[None, :] + identity
    off_diagonal = weights[:, None] / weights[None, :] * parity / spacing * (1.0 - identity)
    return off_diagonal - identity * off_diagonal.sum(axis=1)[:, None]


def halves(table):
    table = np.asarray(table, np.float32)
    high = table.astype(bf16)
    low = (table - high.astype(np.float32)).astype(bf16)
    return high, low


def spanwise_tables():
    rows = np.arange(KZ)
    wavenumber = rows // 2
    product = (np.arange(NZ)[:, None] * wavenumber[None, :]) % NZ
    phase = 2.0 * math.pi / NZ * product
    sine = (rows % 2 == 1)[None, :]
    rate = 4.0 * wavenumber / MODES
    basis = np.where(sine, np.sin(phase), np.cos(phase))
    slope = np.where(sine, rate * np.cos(phase), -rate * np.sin(phase))
    forward = basis.T * np.where(rows == 0, 1.0 / NZ, 2.0 / NZ)[:, None]

    def left(table):
        high, low = halves(table)
        return np.concatenate([high, low, high], axis=1)

    return left(basis), left(slope), left(forward)


def slope_weights():
    chebyshev = chebyshev_matrix()
    along_xi = np.kron(np.eye(8), chebyshev.T)
    along_eta = np.kron(chebyshev.T, np.eye(8))
    both = np.concatenate([np.kron(np.eye(2), along_xi), np.kron(np.eye(2), along_eta)], axis=1)
    high, low = halves(both)
    return np.stack([high, low])


def split(value):
    high = value.astype(bf16).astype(f32)
    return high, value - high


def stacked(value):
    return jnp.concatenate(split(value), axis=0).astype(bf16)


def folded(value):
    half = value.shape[0] // 2
    return value[:half] + value[half:]


def dot(a, b):
    return jnp.dot(a, b, preferred_element_type=f32)


def lanes(shape):
    return lax.broadcasted_iota(jnp.int32, shape, len(shape) - 1)


def pick(value, chooser):
    return folded(dot(stacked(value), chooser))


def scatter(trace, spreader):
    high, low = split(trace)
    return dot((high + pltpu.roll(low, 64, 1)).astype(bf16), spreader)


def both(value, table_ref):
    rows = stacked(value)
    return folded(dot(rows, table_ref[0]) + dot(rows, table_ref[1]))


def mode_rows(value, k):
    return value[SLOT * k : SLOT * (k + 1)]


def turned(value, start, stop):
    parts = []
    for k in range(4):
        by = (stop(k) - start(k)) % 128
        rows = mode_rows(value, k)
        parts.append(pltpu.roll(rows, by, 1) if by else rows)
    return jnp.concatenate(parts, axis=0)


def own_block():
    return lanes((32, 128)) // TRACE == lax.broadcasted_iota(jnp.int32, (32, 128), 0) // SLOT


def blocked(value, lane):
    return jnp.where(own_block(), turned(value, lambda k: lane, lambda k: TRACE * k), 0.0)


def unblocked(value, lane):
    return turned(jnp.where(own_block(), value, 0.0), lambda k: TRACE * k, lambda k: lane)


def pack_points(fields, send_ref):
    first_half = lanes((8, 128)) < 64
    for t in range(8):
        c0, c1, c2 = [fields[c][:, 128 * t : 128 * (t + 1)] for c in range(3)]
        send_ref[2 * t, 0] = jnp.where(first_half, c0, pltpu.roll(c1, 64, 1))
        send_ref[2 * t + 1, 0] = jnp.where(first_half, pltpu.roll(c0, 64, 1), c1)
        send_ref[2 * t, 1] = jnp.where(first_half, c2, 0.0)
        send_ref[2 * t + 1, 1] = jnp.where(first_half, pltpu.roll(c2, 64, 1), 0.0)


def start_kernel(velocity_ref, send_ref, state_ref):
    pack_points([velocity_ref[c] for c in range(3)], send_ref)
    state_ref[...] = jnp.zeros_like(state_ref)
    width = state_ref.shape[2]
    for q in range(state_ref.shape[0]):
        for k in range(4):
            for c in range(3):
                state_ref[q, SLOT * k + 2 * c : SLOT * k + 2 * c + 2, :] = velocity_ref[
                    c, 2 * k : 2 * k + 2, width * q : width * (q + 1)
                ]


def setup_kernel(
    index_ref, maps_ref, mass_ref, main_ref, cross_ref, slopes_ref, basis_ref, slope_ref, forward_ref,
    spreader_ref, chooser_ref, lane_chooser_ref, weight_ref, gate_ref, row_mass_ref, damped_ref, metric_ref,
    slopes_out, basis_out, slope_out, forward_out,
):
    mode, elem, last = index_ref[0], index_ref[1], index_ref[2]
    width = spreader_ref.shape[2]
    lower = jnp.where(elem > 0, 1.0, 0.0)
    upper = jnp.where(elem < last, 1.0, 0.0)
    gate_ref[0:1] = jnp.full((1, 128), lower, f32)
    gate_ref[1:2] = jnp.full((1, 128), upper, f32)
    diagonal = lax.broadcasted_iota(jnp.int32, (128, 128), 0) == lanes((128, 128))
    across = lanes((128, width)).astype(f32)
    along = lax.broadcasted_iota(jnp.int32, (width, 128), 0).astype(f32)
    rows = lax.broadcasted_iota(jnp.int32, (32, width), 0) // SLOT + 4 * mode
    wave = (4.0 / MODES) * rows.astype(f32)
    damping = 1.0 + viscous_step * wave * wave
    for q in range(2):
        column = jnp.sum(jnp.where(diagonal, maps_ref[q : q + 1], 0.0), axis=1, keepdims=True)
        spread = (column == across).astype(f32)
        spreader_ref[q] = spread.astype(bf16)
        chooser_ref[q] = (maps_ref[2 + q : 3 + q] == along).astype(f32).astype(bf16)
        lane_chooser_ref[q] = (maps_ref[4 + q : 5 + q] == along).astype(f32).astype(bf16)
        first = jnp.sum(spread[0:TRACE], axis=0, keepdims=True)
        second = jnp.sum(spread[TRACE : 2 * TRACE], axis=0, keepdims=True)
        first = first * lower if q == 0 else first
        second = second * upper if q == 1 else second
        multiplicity = 1.0 + first + second
        weight_ref[q] = relaxation / (multiplicity * multiplicity)
        mass = jnp.concatenate([mass_ref[4 * q + i : 4 * q + i + 1] for i in range(4)], axis=1)
        row_mass_ref[q] = mass
        damped_ref[q] = damping * mass
    share = lax.rem(1024 - 64 * mode, 1024)
    first_half = lanes((2, 128)) < 64
    for start, ref in ((0, main_ref), (2, cross_ref)):
        part = pltpu.roll(ref[...], share, 1)[:, :128]
        metric_ref[start : start + 2] = jnp.where(first_half, part, pltpu.roll(part, 64, 1))
    slopes_out[...] = slopes_ref[...]
    basis_out[...] = basis_ref[...]
    slope_out[...] = slope_ref[...]
    forward_out[...] = forward_ref[...]


def advection_kernel(seen_ref, metric_ref, slopes_ref, basis_ref, slope_ref, forward_ref, send_ref):
    first_half = lanes((KZ, 128)) < 64
    field01 = seen_ref[:, 0].reshape(KZ, 128)
    field2 = seen_ref[:, 1].reshape(KZ, 128)
    fields = jnp.concatenate([field01, field2], axis=0)
    slopes = both(fields, slopes_ref)
    xi, eta = slopes[:, :128], slopes[:, 128:]
    grad_x = metric_ref[0:1] * xi + metric_ref[2:3] * eta
    grad_y = metric_ref[3:4] * xi + metric_ref[1:2] * eta
    other01 = pltpu.roll(field01, 64, 1)
    speed_u = jnp.where(first_half, field01, other01)
    speed_v = jnp.where(first_half, other01, field01)
    speed_w = jnp.where(first_half, field2, pltpu.roll(field2, 64, 1))

    def right(value):
        high, low = split(value)
        high = high.astype(bf16)
        return jnp.concatenate([high, high, low.astype(bf16)], axis=0)

    def physical(table_ref, value):
        return dot(table_ref[...], right(value))

    speeds = [physical(basis_ref, value) for value in (speed_u, speed_v, speed_w)]
    for part in range(2):
        keep = slice(KZ * part, KZ * (part + 1))
        advection = (
            speeds[0] * physical(basis_ref, grad_x[keep])
            + speeds[1] * physical(basis_ref, grad_y[keep])
            + speeds[2] * physical(slope_ref, fields[keep])
        )
        send_ref[:, part] = dot(forward_ref[...], right(advection)).reshape(16, 8, 128)


def table_kernel(
    precond_ref, stiffness_ref, chooser_ref, lane_chooser_ref, spreader_ref,
    inverse_ref, stiff_ref, column_ref, corner_ref, message_ref, reach_ref, inner_ref,
):
    k = pl.program_id(0)
    width = stiff_ref.shape[2]
    block = pl.ds(pl.multiple_of(TRACE * k, TRACE), TRACE)
    mine = lanes((width, 128)) // TRACE == k

    @pl.when(k == 0)
    def _():
        for q in range(2):
            for part, value in enumerate(split(viscous_step * stiffness_ref[width * q : width * (q + 1)])):
                stiff_ref[q, part] = value.astype(bf16)
        reach_ref[...] = jnp.zeros_like(reach_ref)

    for q in range(2):
        parts = [value.astype(bf16) for value in split(precond_ref[0, width * q : width * (q + 1)].T)]
        spreader = spreader_ref[q, TRACE * q : TRACE * (q + 1)]
        lane_chooser = jnp.where(mine, lane_chooser_ref[q].astype(f32), 0.0).astype(bf16)
        facing = spreader_ref[q, TRACE * (1 - q) : TRACE * (2 - q)]
        corner = inner = 0.0
        for part in range(2):
            inverse_ref[k, q, part] = parts[part]
            column = dot(spreader, parts[part]).astype(bf16)
            column_ref[q, part, block] = column
            corner = corner + dot(column, chooser_ref[q])
            inner = inner + dot(dot(facing, parts[part]).astype(bf16), chooser_ref[q])
            reach = dot(parts[part], lane_chooser)
            reach_ref[q, part] = (reach_ref[q, part].astype(f32) + reach).astype(bf16)
        message_ref[q, block] = corner
        for part, value in enumerate(split(corner)):
            corner_ref[q, part, block] = value.astype(bf16)
        for part, value in enumerate(split(inner)):
            inner_ref[q, part, block] = value.astype(bf16)


def link_kernel(lower_ref, upper_ref, gate_ref, link_ref):
    for q, ref in enumerate((lower_ref, upper_ref)):
        for part, value in enumerate(split(ref[32:160] * gate_ref[q : q + 1])):
            link_ref[q, part] = value.astype(bf16)


def send_traces(residual, reach_ref, inner_ref, chooser_ref, trace_ref, up_ref, down_ref):
    trace = [pick(residual[q], chooser_ref[q]) for q in range(2)]
    for q in range(2):
        trace_ref[q] = trace[q]
        reached = unblocked(both(residual[q], reach_ref.at[q]), 96 if q == 0 else 64)
        facing = both(blocked(trace[1 - q], TRACE * (1 - q)), inner_ref.at[q])
        upper_half = lanes((32, 128)) >= 64
        facing = jnp.where(upper_half, pltpu.roll(facing, 64, 1), 0.0)
        (down_ref, up_ref)[q][0:32] = trace[q] + reached + facing


def precondition_kernel(
    residual_ref, seen_ref, inverse_ref, chooser_ref, spreader_ref, part_ref, trace_ref, gained_ref
):
    lane = lanes((32, 128))
    inner = [
        jnp.where((lane >= TRACE) & (lane < 2 * TRACE), seen_ref[1], 0.0),
        jnp.where(lane < TRACE, seen_ref[0], 0.0),
    ]
    for q in range(2):
        gained_ref[q] = residual_ref[q] + scatter(inner[q], spreader_ref[q])

    def one_mode(k, carry):
        rows = pl.ds(pl.multiple_of(SLOT * k, SLOT), SLOT)
        for q in range(2):
            part_ref[q, rows] = both(gained_ref[q, rows], inverse_ref.at[k, q])
        return carry

    lax.fori_loop(0, 4, one_mode, 0)
    for q in range(2):
        trace_ref[q] = pick(part_ref[q], chooser_ref[q])


def first_kernel(
    seen_ref, state_ref, mass_ref, reach_ref, inner_ref, chooser_ref, *refs
):
    refs = list(refs)
    corners_ref = refs.pop(0) if len(refs) > 4 else None
    local_ref, trace_ref, up_ref, down_ref = refs
    first_half = lanes((8, 128)) < 64
    local_ref[...] = jnp.zeros_like(local_ref)
    per_patch = local_ref.shape[2] // 128
    for t in range(8):
        a0, b0 = seen_ref[2 * t, 0], seen_ref[2 * t + 1, 0]
        a1, b1 = seen_ref[2 * t, 1], seen_ref[2 * t + 1, 1]
        fields = [
            jnp.where(first_half, a0, pltpu.roll(b0, 64, 1)),
            jnp.where(first_half, pltpu.roll(a0, 64, 1), b0),
            jnp.where(first_half, a1, pltpu.roll(b1, 64, 1)),
        ]
        where = slice(128 * (t % per_patch), 128 * (t % per_patch + 1))
        for k in range(4):
            for c in range(3):
                local_ref[t // per_patch, SLOT * k + 2 * c : SLOT * k + 2 * c + 2, where] = fields[c][
                    2 * k : 2 * k + 2
                ]
    local = [mass_ref[q] * (state_ref[q] - time_step * local_ref[q]) for q in range(2)]
    for q in range(2):
        local_ref[q] = local[q]
    send_traces(local, reach_ref, inner_ref, chooser_ref, trace_ref, up_ref, down_ref)
    if corners_ref is not None:
        down_ref[32:160] = corners_ref[0]
        up_ref[32:160] = corners_ref[1]


def update(
    lower_ref, upper_ref, part_ref, part_trace_ref, trace_ref, gate_ref, weight_ref, column_ref,
    corner_ref, link_ref, spreader_ref,
):
    lane = lanes((32, 128))
    low = lane < TRACE
    high = (lane >= TRACE) & (lane < 2 * TRACE)
    lower = jnp.where(gate_ref[0:1] > 0.0, lower_ref[0:32], 0.0)
    upper = jnp.where(gate_ref[1:2] > 0.0, upper_ref[0:32], 0.0)
    inflow = [blocked(lower, 0), blocked(upper, TRACE)]
    linked = [both(blocked(trace_ref[q], TRACE * (1 - q)), link_ref.at[q]) for q in range(2)]
    inner = [part_trace_ref[q] + both(inflow[q], corner_ref.at[q]) for q in range(2)]
    gains = [
        jnp.where(low, pltpu.roll(lower, 64, 1) + linked[0], jnp.where(high, inner[1], 0.0)),
        jnp.where(high, pltpu.roll(upper, 64, 1) + linked[1], jnp.where(low, inner[0], 0.0)),
    ]
    return [
        weight_ref[q]
        * (part_ref[q] + both(inflow[q], column_ref.at[q]) + scatter(gains[q], spreader_ref[q]))
        for q in range(2)
    ]


def sweep_kernel(fresh, *refs):
    refs = list(refs)
    iterate_ref = None if fresh else refs.pop(0)
    received, refs = refs[:11], refs[11:]
    (
        local_ref, chooser_ref, damped_ref, stiff_ref, reach_ref, inner_ref,
        next_ref, residual_ref, trace_ref, up_ref, down_ref,
    ) = refs
    step = update(*received)
    residual = []
    for q in range(2):
        iterate = step[q] if fresh else iterate_ref[q] + step[q]
        next_ref[q] = iterate
        residual.append(local_ref[q] - both(iterate, stiff_ref.at[q]) - damped_ref[q] * iterate)
        residual_ref[q] = residual[q]
    send_traces(residual, reach_ref, inner_ref, chooser_ref, trace_ref, up_ref, down_ref)


def last_kernel(final, iterate_ref, *refs):
    received, outs = refs[:11], refs[11:]
    step = update(*received)
    state = [iterate_ref[q] + step[q] for q in range(2)]
    field_ref = outs[0] if final else outs[2]
    width = state[0].shape[1]
    for q in range(2):
        for k in range(4):
            for c in range(3):
                field_ref[c, 2 * k : 2 * k + 2, width * q : width * (q + 1)] = state[q][
                    SLOT * k + 2 * c : SLOT * k + 2 * c + 2
                ]
    if not final:
        send_ref, state_ref = outs[0], outs[1]
        for q in range(2):
            state_ref[q] = state[q]
        pack_points([field_ref[c] for c in range(3)], send_ref)


VMEM = pl.BlockSpec(memory_space=pltpu.VMEM)
SCOPED = 24 << 20


def call(kernel, outs, *args, scratch=(), name=None, flops=0):
    single = not isinstance(outs, (list, tuple))
    shapes = [outs] if single else list(outs)
    cost = pl.CostEstimate(flops=flops, bytes_accessed=0, transcendentals=0) if flops else None
    return pl.pallas_call(
        kernel,
        out_shape=shapes[0] if single else shapes,
        in_specs=[VMEM] * len(args),
        out_specs=VMEM if single else [VMEM] * len(shapes),
        scratch_shapes=list(scratch),
        name=name,
        cost_estimate=cost,
        compiler_params=pltpu.CompilerParams(vmem_limit_bytes=SCOPED),
    )(*args)


def in_hbm(value):
    return pltpu.with_memory_space_constraint(value, pltpu.HBM)


def shape(*dims, dtype=f32):
    return jax.ShapeDtypeStruct(dims, dtype)


def on_device(velocity, metric_main, metric_cross, stiffness, mass, precond, trace_map):
    points = velocity.shape[2]
    width = stiffness.shape[1]
    patches = trace_map.shape[0]
    mode_count = lax.axis_size("mode")
    elem_count = lax.axis_size("elem")
    mode_index = lax.axis_index("mode")
    elem_index = lax.axis_index("elem")
    share = points // mode_count

    packed = shape(16, 2, 8, 128)
    solver = shape(2, 32, width)
    trace_pair = shape(2, 32, 128)
    message = shape(32, 128)
    send, state = call(start_kernel, [packed, solver], in_hbm(velocity), name="start")

    lower_map, upper_map = [trace_map[:, side].astype(f32) for side in range(2)]
    nowhere = jnp.full_like(lower_map, -1.0)
    maps = jnp.concatenate(
        [
            jnp.concatenate([lower_map, upper_map, lower_map, upper_map], axis=1),
            jnp.concatenate([upper_map, lower_map, nowhere, nowhere], axis=1),
            jnp.tile(jnp.stack([lower_map[0], upper_map[1]]), (1, 4)),
        ]
    )
    index = jnp.stack([mode_index, elem_index, jnp.full_like(elem_index, elem_count - 1)])
    tables = [jnp.asarray(table) for table in (slope_weights(), *spanwise_tables())]
    small = [
        shape(patches, 128, width, dtype=bf16),
        shape(patches, width, 128, dtype=bf16),
        shape(patches, width, 128, dtype=bf16),
        shape(patches, 1, width),
        shape(2, 128),
        shape(patches, 1, width),
        shape(patches, 32, width),
        shape(4, 128),
    ] + [shape(*table.shape, dtype=bf16) for table in tables]
    (
        spreader, chooser, lane_chooser, weight, gate, patch_mass, damped, metric,
        slopes, basis, slope, forward,
    ) = pl.pallas_call(
        setup_kernel,
        out_shape=small,
        in_specs=[pl.BlockSpec(memory_space=pltpu.SMEM)] + [VMEM] * 8,
        out_specs=[VMEM] * 12,
        name="setup",
        compiler_params=pltpu.CompilerParams(vmem_limit_bytes=SCOPED),
    )(index, maps, *[in_hbm(value) for value in (mass.reshape(8, -1), metric_main, metric_cross, *tables)])

    up = [(i, (i + 1) % elem_count) for i in range(elem_count)]
    down = [((i + 1) % elem_count, i) for i in range(elem_count)]

    def neighbours(upward, downward):
        return lax.ppermute(upward, "elem", up), lax.ppermute(downward, "elem", down)

    def transpose(value):
        return lax.all_to_all(value, "mode", split_axis=0, concat_axis=0, tiled=True)

    def precondition(residual, trace):
        return call(
            precondition_kernel, [solver, trace_pair], residual, trace, inverse, chooser, spreader,
            scratch=[pltpu.VMEM((2, 32, width), f32)],
            name="precondition", flops=8 * 4 * 2 * 16 * width * width,
        )

    for time_level in range(STEPS):
        send = call(
            advection_kernel, packed, transpose(send), metric, slopes, basis, slope, forward, name="advection"
        )
        seen = transpose(send)
        opening = time_level == 0
        if opening:
            seen, precond = lax.optimization_barrier((seen, precond))
            inverse, stiff, column, corner, corners, reach, inner = pl.pallas_call(
                table_kernel,
                grid=(4,),
                out_shape=[
                    shape(4, 2, 2, width, width, dtype=bf16),
                    shape(2, 2, width, width, dtype=bf16),
                    shape(2, 2, 128, width, dtype=bf16),
                    shape(2, 2, 128, 128, dtype=bf16),
                    shape(2, 128, 128),
                    shape(2, 2, width, 128, dtype=bf16),
                shape(2, 2, 128, 128, dtype=bf16),
                ],
                in_specs=[pl.BlockSpec((1, patches * width, width), lambda k: (k, 0, 0))] + [VMEM] * 4,
                out_specs=[VMEM] * 7,
                name="tables",
                compiler_params=pltpu.CompilerParams(vmem_limit_bytes=SCOPED),
            )(in_hbm(precond), in_hbm(stiffness), chooser, lane_chooser, spreader)
        sent = shape(160, 128) if opening else message
        local, trace, upward, downward = call(
            first_kernel, [solver, trace_pair, sent, sent],
            seen, state, patch_mass, reach, inner, chooser,
            *((corners,) if opening else ()), name="first",
        )
        iterate, residual = (), local
        for sweep_number in range(ITERS):
            lower, upper = neighbours(upward, downward)
            part, part_trace = precondition(residual, trace)
            if opening and sweep_number == 0:
                link = call(
                    link_kernel, shape(2, 2, 128, 128, dtype=bf16), lower, upper, gate, name="links"
                )
            received = (lower, upper, part, part_trace, trace, gate, weight, column, corner, link, spreader)
            if sweep_number < ITERS - 1:
                iterate, residual, trace, upward, downward = call(
                    functools.partial(sweep_kernel, sweep_number == 0),
                    [solver, solver, trace_pair, message, message],
                    *iterate, *received, local, chooser, damped, stiff, reach, inner, name="sweep",
                )
                iterate = (iterate,)
            elif time_level < STEPS - 1:
                send, state = call(
                    functools.partial(last_kernel, False), [packed, solver], *iterate, *received,
                    scratch=[pltpu.VMEM((3, 8, points), f32)], name="last",
                )
            else:
                state = call(
                    functools.partial(last_kernel, True), shape(3, 8, points), *iterate, *received, name="final"
                )
    return state


def solution(mesh):
    return jax.shard_map(
        on_device,
        mesh=mesh,
        in_specs=(
            P(None, "mode", "elem"),
            P(None, "elem"),
            P(None, "elem"),
            P("elem", None),
            P("elem"),
            P("mode", "elem", None),
            P("elem", None, None),
        ),
        out_specs=P(None, "mode", "elem"),
        check_vma=False,
    )
```

```python
import functools
import math

import jax
import jax.numpy as jnp
import numpy as np
from jax import lax
from jax.experimental import pallas as pl
from jax.experimental.pallas import tpu as pltpu
from jax.sharding import PartitionSpec as P

MODES = 64
KZ = 128
NZ = 256
STEPS = 4
ITERS = 4
TRACE = 32
SLOT = 8

viscous_step = 0.5
time_step = 0.02
relaxation = 0.8

f32 = jnp.float32
bf16 = jnp.bfloat16


def chebyshev_matrix():
    node_points = np.cos(np.pi * np.arange(8) / 7.0)
    weights = np.where((np.arange(8) == 0) | (np.arange(8) == 7), 2.0, 1.0)
    parity = np.where((np.arange(8)[:, None] + np.arange(8)[None, :]) % 2 == 0, 1.0, -1.0)
    identity = np.eye(8)
    spacing = node_points[:, None] - node_points[None, :] + identity
    off_diagonal = weights[:, None] / weights[None, :] * parity / spacing * (1.0 - identity)
    return off_diagonal - identity * off_diagonal.sum(axis=1)[:, None]


def halves(table):
    table = np.asarray(table, np.float32)
    high = table.astype(bf16)
    low = (table - high.astype(np.float32)).astype(bf16)
    return high, low


def spanwise_tables():
    rows = np.arange(KZ)
    wavenumber = rows // 2
    product = (np.arange(NZ)[:, None] * wavenumber[None, :]) % NZ
    phase = 2.0 * math.pi / NZ * product
    sine = (rows % 2 == 1)[None, :]
    rate = 4.0 * wavenumber / MODES
    basis = np.where(sine, np.sin(phase), np.cos(phase))
    slope = np.where(sine, rate * np.cos(phase), -rate * np.sin(phase))
    forward = basis.T * np.where(rows == 0, 1.0 / NZ, 2.0 / NZ)[:, None]

    def left(table):
        high, low = halves(table)
        return np.concatenate([high, low, high], axis=1)

    return left(basis), left(slope), left(forward)


def slope_weights():
    chebyshev = chebyshev_matrix()
    along_xi = np.kron(np.eye(8), chebyshev.T)
    along_eta = np.kron(chebyshev.T, np.eye(8))
    both = np.concatenate([np.kron(np.eye(2), along_xi), np.kron(np.eye(2), along_eta)], axis=1)
    high, low = halves(both)
    return np.stack([high, low])


def split(value):
    high = value.astype(bf16).astype(f32)
    return high, value - high


def stacked(value):
    return jnp.concatenate(split(value), axis=0).astype(bf16)


def folded(value):
    half = value.shape[0] // 2
    return value[:half] + value[half:]


def dot(a, b):
    return jnp.dot(a, b, preferred_element_type=f32)


def lanes(shape):
    return lax.broadcasted_iota(jnp.int32, shape, len(shape) - 1)


def pick(value, chooser):
    return folded(dot(stacked(value), chooser))


def scatter(trace, spreader):
    high, low = split(trace)
    return dot((high + pltpu.roll(low, 64, 1)).astype(bf16), spreader)


def both(value, table_ref):
    rows = stacked(value)
    return folded(dot(rows, table_ref[0]) + dot(rows, table_ref[1]))


def mode_rows(value, k):
    return value[SLOT * k : SLOT * (k + 1)]


def turned(value, start, stop):
    parts = []
    for k in range(4):
        by = (stop(k) - start(k)) % 128
        rows = mode_rows(value, k)
        parts.append(pltpu.roll(rows, by, 1) if by else rows)
    return jnp.concatenate(parts, axis=0)


def own_block():
    return lanes((32, 128)) // TRACE == lax.broadcasted_iota(jnp.int32, (32, 128), 0) // SLOT


def blocked(value, lane):
    return jnp.where(own_block(), turned(value, lambda k: lane, lambda k: TRACE * k), 0.0)


def unblocked(value, lane):
    return turned(jnp.where(own_block(), value, 0.0), lambda k: TRACE * k, lambda k: lane)


def pack_points(fields, send_ref):
    first_half = lanes((8, 128)) < 64
    for t in range(8):
        c0, c1, c2 = [fields[c][:, 128 * t : 128 * (t + 1)] for c in range(3)]
        send_ref[2 * t, 0] = jnp.where(first_half, c0, pltpu.roll(c1, 64, 1))
        send_ref[2 * t + 1, 0] = jnp.where(first_half, pltpu.roll(c0, 64, 1), c1)
        send_ref[2 * t, 1] = jnp.where(first_half, c2, 0.0)
        send_ref[2 * t + 1, 1] = jnp.where(first_half, pltpu.roll(c2, 64, 1), 0.0)


def start_kernel(velocity_ref, send_ref, state_ref):
    pack_points([velocity_ref[c] for c in range(3)], send_ref)
    state_ref[...] = jnp.zeros_like(state_ref)
    width = state_ref.shape[2]
    for q in range(state_ref.shape[0]):
        for k in range(4):
            for c in range(3):
                state_ref[q, SLOT * k + 2 * c : SLOT * k + 2 * c + 2, :] = velocity_ref[
                    c, 2 * k : 2 * k + 2, width * q : width * (q + 1)
                ]


def setup_kernel(
    index_ref, maps_ref, mass_ref, main_ref, cross_ref, slopes_ref, basis_ref, slope_ref, forward_ref,
    spreader_ref, chooser_ref, lane_chooser_ref, weight_ref, gate_ref, row_mass_ref, damped_ref, metric_ref,
    slopes_out, basis_out, slope_out, forward_out,
):
    mode, elem, last = index_ref[0], index_ref[1], index_ref[2]
    width = spreader_ref.shape[2]
    lower = jnp.where(elem > 0, 1.0, 0.0)
    upper = jnp.where(elem < last, 1.0, 0.0)
    gate_ref[0:1] = jnp.full((1, 128), lower, f32)
    gate_ref[1:2] = jnp.full((1, 128), upper, f32)
    diagonal = lax.broadcasted_iota(jnp.int32, (128, 128), 0) == lanes((128, 128))
    across = lanes((128, width)).astype(f32)
    along = lax.broadcasted_iota(jnp.int32, (width, 128), 0).astype(f32)
    rows = lax.broadcasted_iota(jnp.int32, (32, width), 0) // SLOT + 4 * mode
    wave = (4.0 / MODES) * rows.astype(f32)
    damping = 1.0 + viscous_step * wave * wave
    for q in range(2):
        column = jnp.sum(jnp.where(diagonal, maps_ref[q : q + 1], 0.0), axis=1, keepdims=True)
        spread = (column == across).astype(f32)
        spreader_ref[q] = spread.astype(bf16)
        chooser_ref[q] = (maps_ref[2 + q : 3 + q] == along).astype(f32).astype(bf16)
        lane_chooser_ref[q] = (maps_ref[4 + q : 5 + q] == along).astype(f32).astype(bf16)
        first = jnp.sum(spread[0:TRACE], axis=0, keepdims=True)
        second = jnp.sum(spread[TRACE : 2 * TRACE], axis=0, keepdims=True)
        first = first * lower if q == 0 else first
        second = second * upper if q == 1 else second
        multiplicity = 1.0 + first + second
        weight_ref[q] = relaxation / (multiplicity * multiplicity)
        mass = jnp.concatenate([mass_ref[4 * q + i : 4 * q + i + 1] for i in range(4)], axis=1)
        row_mass_ref[q] = mass
        damped_ref[q] = damping * mass
    share = lax.rem(1024 - 64 * mode, 1024)
    first_half = lanes((2, 128)) < 64
    for start, ref in ((0, main_ref), (2, cross_ref)):
        part = pltpu.roll(ref[...], share, 1)[:, :128]
        metric_ref[start : start + 2] = jnp.where(first_half, part, pltpu.roll(part, 64, 1))
    slopes_out[...] = slopes_ref[...]
    basis_out[...] = basis_ref[...]
    slope_out[...] = slope_ref[...]
    forward_out[...] = forward_ref[...]


def advection_kernel(seen_ref, metric_ref, slopes_ref, basis_ref, slope_ref, forward_ref, send_ref):
    first_half = lanes((KZ, 128)) < 64
    field01 = seen_ref[:, 0].reshape(KZ, 128)
    field2 = seen_ref[:, 1].reshape(KZ, 128)
    fields = jnp.concatenate([field01, field2], axis=0)
    slopes = both(fields, slopes_ref)
    xi, eta = slopes[:, :128], slopes[:, 128:]
    grad_x = metric_ref[0:1] * xi + metric_ref[2:3] * eta
    grad_y = metric_ref[3:4] * xi + metric_ref[1:2] * eta
    other01 = pltpu.roll(field01, 64, 1)
    speed_u = jnp.where(first_half, field01, other01)
    speed_v = jnp.where(first_half, other01, field01)
    speed_w = jnp.where(first_half, field2, pltpu.roll(field2, 64, 1))

    def right(value):
        high, low = split(value)
        high = high.astype(bf16)
        return jnp.concatenate([high, high, low.astype(bf16)], axis=0)

    def physical(table_ref, value):
        return dot(table_ref[...], right(value))

    speeds = [physical(basis_ref, value) for value in (speed_u, speed_v, speed_w)]
    for part in range(2):
        keep = slice(KZ * part, KZ * (part + 1))
        advection = (
            speeds[0] * physical(basis_ref, grad_x[keep])
            + speeds[1] * physical(basis_ref, grad_y[keep])
            + speeds[2] * physical(slope_ref, fields[keep])
        )
        send_ref[:, part] = dot(forward_ref[...], right(advection)).reshape(16, 8, 128)


def table_kernel(
    precond_ref, stiffness_ref, chooser_ref, lane_chooser_ref, spreader_ref,
    inverse_ref, stiff_ref, column_ref, corner_ref, message_ref, reach_ref, inner_ref,
):
    k = pl.program_id(0)
    width = stiff_ref.shape[2]
    block = pl.ds(pl.multiple_of(TRACE * k, TRACE), TRACE)
    mine = lanes((width, 128)) // TRACE == k

    @pl.when(k == 0)
    def _():
        for q in range(2):
            for part, value in enumerate(split(viscous_step * stiffness_ref[width * q : width * (q + 1)])):
                stiff_ref[q, part] = value.astype(bf16)
        reach_ref[...] = jnp.zeros_like(reach_ref)

    for q in range(2):
        parts = [value.astype(bf16) for value in split(precond_ref[0, width * q : width * (q + 1)].T)]
        mine_rows = slice(TRACE * q, TRACE * (q + 1))
        facing_rows = slice(TRACE * (1 - q), TRACE * (2 - q))
        lane_chooser = jnp.where(mine, lane_chooser_ref[q].astype(f32), 0.0).astype(bf16)
        corners = 0.0
        for part in range(2):
            inverse_ref[k, q, part] = parts[part]
            columns = dot(spreader_ref[q, 0 : 2 * TRACE], parts[part])
            column_ref[q, part, block] = columns[mine_rows].astype(bf16)
            corners = corners + dot(columns.astype(bf16), chooser_ref[q])
            reach = dot(parts[part], lane_chooser)
            reach_ref[q, part] = (reach_ref[q, part].astype(f32) + reach).astype(bf16)
        message_ref[q, block] = corners[mine_rows]
        for part, value in enumerate(split(corners[mine_rows])):
            corner_ref[q, part, block] = value.astype(bf16)
        for part, value in enumerate(split(corners[facing_rows])):
            inner_ref[q, part, block] = value.astype(bf16)


def link_kernel(lower_ref, upper_ref, gate_ref, link_ref):
    for q, ref in enumerate((lower_ref, upper_ref)):
        for part, value in enumerate(split(ref[32:160] * gate_ref[q : q + 1])):
            link_ref[q, part] = value.astype(bf16)


def send_traces(residual, reach_ref, inner_ref, chooser_ref, trace_ref, up_ref, down_ref):
    trace = [pick(residual[q], chooser_ref[q]) for q in range(2)]
    for q in range(2):
        trace_ref[q] = trace[q]
        reached = unblocked(both(residual[q], reach_ref.at[q]), 96 if q == 0 else 64)
        facing = both(blocked(trace[1 - q], TRACE * (1 - q)), inner_ref.at[q])
        upper_half = lanes((32, 128)) >= 64
        facing = jnp.where(upper_half, pltpu.roll(facing, 64, 1), 0.0)
        (down_ref, up_ref)[q][0:32] = trace[q] + reached + facing


def precondition_kernel(
    residual_ref, seen_ref, inverse_ref, chooser_ref, spreader_ref, part_ref, trace_ref, gained_ref
):
    lane = lanes((32, 128))
    inner = [
        jnp.where((lane >= TRACE) & (lane < 2 * TRACE), seen_ref[1], 0.0),
        jnp.where(lane < TRACE, seen_ref[0], 0.0),
    ]
    for q in range(2):
        gained_ref[q] = residual_ref[q] + scatter(inner[q], spreader_ref[q])

    def one_mode(k, carry):
        rows = pl.ds(pl.multiple_of(SLOT * k, SLOT), SLOT)
        for q in range(2):
            part_ref[q, rows] = both(gained_ref[q, rows], inverse_ref.at[k, q])
        return carry

    lax.fori_loop(0, 4, one_mode, 0)
    for q in range(2):
        trace_ref[q] = pick(part_ref[q], chooser_ref[q])


def first_kernel(
    seen_ref, state_ref, mass_ref, reach_ref, inner_ref, chooser_ref, *refs
):
    refs = list(refs)
    corners_ref = refs.pop(0) if len(refs) > 4 else None
    local_ref, trace_ref, up_ref, down_ref = refs
    first_half = lanes((8, 128)) < 64
    local_ref[...] = jnp.zeros_like(local_ref)
    per_patch = local_ref.shape[2] // 128
    for t in range(8):
        a0, b0 = seen_ref[2 * t, 0], seen_ref[2 * t + 1, 0]
        a1, b1 = seen_ref[2 * t, 1], seen_ref[2 * t + 1, 1]
        fields = [
            jnp.where(first_half, a0, pltpu.roll(b0, 64, 1)),
            jnp.where(first_half, pltpu.roll(a0, 64, 1), b0),
            jnp.where(first_half, a1, pltpu.roll(b1, 64, 1)),
        ]
        where = slice(128 * (t % per_patch), 128 * (t % per_patch + 1))
        for k in range(4):
            for c in range(3):
                local_ref[t // per_patch, SLOT * k + 2 * c : SLOT * k + 2 * c + 2, where] = fields[c][
                    2 * k : 2 * k + 2
                ]
    local = [mass_ref[q] * (state_ref[q] - time_step * local_ref[q]) for q in range(2)]
    for q in range(2):
        local_ref[q] = local[q]
    send_traces(local, reach_ref, inner_ref, chooser_ref, trace_ref, up_ref, down_ref)
    if corners_ref is not None:
        down_ref[32:160] = corners_ref[0]
        up_ref[32:160] = corners_ref[1]


def update(
    lower_ref, upper_ref, part_ref, part_trace_ref, trace_ref, gate_ref, weight_ref, column_ref,
    corner_ref, link_ref, spreader_ref,
):
    lane = lanes((32, 128))
    low = lane < TRACE
    high = (lane >= TRACE) & (lane < 2 * TRACE)
    lower = jnp.where(gate_ref[0:1] > 0.0, lower_ref[0:32], 0.0)
    upper = jnp.where(gate_ref[1:2] > 0.0, upper_ref[0:32], 0.0)
    inflow = [blocked(lower, 0), blocked(upper, TRACE)]
    linked = [both(blocked(trace_ref[q], TRACE * (1 - q)), link_ref.at[q]) for q in range(2)]
    inner = [part_trace_ref[q] + both(inflow[q], corner_ref.at[q]) for q in range(2)]
    gains = [
        jnp.where(low, pltpu.roll(lower, 64, 1) + linked[0], jnp.where(high, inner[1], 0.0)),
        jnp.where(high, pltpu.roll(upper, 64, 1) + linked[1], jnp.where(low, inner[0], 0.0)),
    ]
    return [
        weight_ref[q]
        * (part_ref[q] + both(inflow[q], column_ref.at[q]) + scatter(gains[q], spreader_ref[q]))
        for q in range(2)
    ]


def sweep_kernel(fresh, *refs):
    refs = list(refs)
    iterate_ref = None if fresh else refs.pop(0)
    received, refs = refs[:11], refs[11:]
    (
        local_ref, chooser_ref, damped_ref, stiff_ref, reach_ref, inner_ref,
        next_ref, residual_ref, trace_ref, up_ref, down_ref,
    ) = refs
    step = update(*received)
    residual = []
    for q in range(2):
        iterate = step[q] if fresh else iterate_ref[q] + step[q]
        next_ref[q] = iterate
        residual.append(local_ref[q] - both(iterate, stiff_ref.at[q]) - damped_ref[q] * iterate)
        residual_ref[q] = residual[q]
    send_traces(residual, reach_ref, inner_ref, chooser_ref, trace_ref, up_ref, down_ref)


def last_kernel(final, iterate_ref, *refs):
    received, outs = refs[:11], refs[11:]
    step = update(*received)
    state = [iterate_ref[q] + step[q] for q in range(2)]
    field_ref = outs[0] if final else outs[2]
    width = state[0].shape[1]
    for q in range(2):
        for k in range(4):
            for c in range(3):
                field_ref[c, 2 * k : 2 * k + 2, width * q : width * (q + 1)] = state[q][
                    SLOT * k + 2 * c : SLOT * k + 2 * c + 2
                ]
    if not final:
        send_ref, state_ref = outs[0], outs[1]
        for q in range(2):
            state_ref[q] = state[q]
        pack_points([field_ref[c] for c in range(3)], send_ref)


VMEM = pl.BlockSpec(memory_space=pltpu.VMEM)
SCOPED = 24 << 20


def call(kernel, outs, *args, scratch=(), name=None, flops=0):
    single = not isinstance(outs, (list, tuple))
    shapes = [outs] if single else list(outs)
    cost = pl.CostEstimate(flops=flops, bytes_accessed=0, transcendentals=0) if flops else None
    return pl.pallas_call(
        kernel,
        out_shape=shapes[0] if single else shapes,
        in_specs=[VMEM] * len(args),
        out_specs=VMEM if single else [VMEM] * len(shapes),
        scratch_shapes=list(scratch),
        name=name,
        cost_estimate=cost,
        compiler_params=pltpu.CompilerParams(vmem_limit_bytes=SCOPED),
    )(*args)


def in_hbm(value):
    return pltpu.with_memory_space_constraint(value, pltpu.HBM)


def shape(*dims, dtype=f32):
    return jax.ShapeDtypeStruct(dims, dtype)


def on_device(velocity, metric_main, metric_cross, stiffness, mass, precond, trace_map):
    points = velocity.shape[2]
    width = stiffness.shape[1]
    patches = trace_map.shape[0]
    mode_count = lax.axis_size("mode")
    elem_count = lax.axis_size("elem")
    mode_index = lax.axis_index("mode")
    elem_index = lax.axis_index("elem")
    share = points // mode_count

    packed = shape(16, 2, 8, 128)
    solver = shape(2, 32, width)
    trace_pair = shape(2, 32, 128)
    message = shape(32, 128)
    send, state = call(start_kernel, [packed, solver], in_hbm(velocity), name="start")

    lower_map, upper_map = [trace_map[:, side].astype(f32) for side in range(2)]
    nowhere = jnp.full_like(lower_map, -1.0)
    maps = jnp.concatenate(
        [
            jnp.concatenate([lower_map, upper_map, lower_map, upper_map], axis=1),
            jnp.concatenate([upper_map, lower_map, nowhere, nowhere], axis=1),
            jnp.tile(jnp.stack([lower_map[0], upper_map[1]]), (1, 4)),
        ]
    )
    index = jnp.stack([mode_index, elem_index, jnp.full_like(elem_index, elem_count - 1)])
    tables = [jnp.asarray(table) for table in (slope_weights(), *spanwise_tables())]
    small = [
        shape(patches, 128, width, dtype=bf16),
        shape(patches, width, 128, dtype=bf16),
        shape(patches, width, 128, dtype=bf16),
        shape(patches, 1, width),
        shape(2, 128),
        shape(patches, 1, width),
        shape(patches, 32, width),
        shape(4, 128),
    ] + [shape(*table.shape, dtype=bf16) for table in tables]
    (
        spreader, chooser, lane_chooser, weight, gate, patch_mass, damped, metric,
        slopes, basis, slope, forward,
    ) = pl.pallas_call(
        setup_kernel,
        out_shape=small,
        in_specs=[pl.BlockSpec(memory_space=pltpu.SMEM)] + [VMEM] * 8,
        out_specs=[VMEM] * 12,
        name="setup",
        compiler_params=pltpu.CompilerParams(vmem_limit_bytes=SCOPED),
    )(index, maps, *[in_hbm(value) for value in (mass.reshape(8, -1), metric_main, metric_cross, *tables)])

    up = [(i, (i + 1) % elem_count) for i in range(elem_count)]
    down = [((i + 1) % elem_count, i) for i in range(elem_count)]

    def neighbours(upward, downward):
        return lax.ppermute(upward, "elem", up), lax.ppermute(downward, "elem", down)

    def transpose(value):
        return lax.all_to_all(value, "mode", split_axis=0, concat_axis=0, tiled=True)

    def precondition(residual, trace):
        return call(
            precondition_kernel, [solver, trace_pair], residual, trace, inverse, chooser, spreader,
            scratch=[pltpu.VMEM((2, 32, width), f32)],
            name="precondition", flops=8 * 4 * 2 * 16 * width * width,
        )

    for time_level in range(STEPS):
        send = call(
            advection_kernel, packed, transpose(send), metric, slopes, basis, slope, forward, name="advection"
        )
        seen = transpose(send)
        opening = time_level == 0
        if opening:
            seen, precond = lax.optimization_barrier((seen, precond))
            inverse, stiff, column, corner, corners, reach, inner = pl.pallas_call(
                table_kernel,
                grid=(4,),
                out_shape=[
                    shape(4, 2, 2, width, width, dtype=bf16),
                    shape(2, 2, width, width, dtype=bf16),
                    shape(2, 2, 128, width, dtype=bf16),
                    shape(2, 2, 128, 128, dtype=bf16),
                    shape(2, 128, 128),
                    shape(2, 2, width, 128, dtype=bf16),
                shape(2, 2, 128, 128, dtype=bf16),
                ],
                in_specs=[pl.BlockSpec((1, patches * width, width), lambda k: (k, 0, 0))] + [VMEM] * 4,
                out_specs=[VMEM] * 7,
                name="tables",
                compiler_params=pltpu.CompilerParams(vmem_limit_bytes=SCOPED),
            )(in_hbm(precond), in_hbm(stiffness), chooser, lane_chooser, spreader)
        sent = shape(160, 128) if opening else message
        local, trace, upward, downward = call(
            first_kernel, [solver, trace_pair, sent, sent],
            seen, state, patch_mass, reach, inner, chooser,
            *((corners,) if opening else ()), name="first",
        )
        iterate, residual = (), local
        for sweep_number in range(ITERS):
            lower, upper = neighbours(upward, downward)
            part, part_trace = precondition(residual, trace)
            if opening and sweep_number == 0:
                link = call(
                    link_kernel, shape(2, 2, 128, 128, dtype=bf16), lower, upper, gate, name="links"
                )
            received = (lower, upper, part, part_trace, trace, gate, weight, column, corner, link, spreader)
            if sweep_number < ITERS - 1:
                iterate, residual, trace, upward, downward = call(
                    functools.partial(sweep_kernel, sweep_number == 0),
                    [solver, solver, trace_pair, message, message],
                    *iterate, *received, local, chooser, damped, stiff, reach, inner, name="sweep",
                )
                iterate = (iterate,)
            elif time_level < STEPS - 1:
                send, state = call(
                    functools.partial(last_kernel, False), [packed, solver], *iterate, *received,
                    scratch=[pltpu.VMEM((3, 8, points), f32)], name="last",
                )
            else:
                state = call(
                    functools.partial(last_kernel, True), shape(3, 8, points), *iterate, *received, name="final"
                )
    return state


def solution(mesh):
    return jax.shard_map(
        on_device,
        mesh=mesh,
        in_specs=(
            P(None, "mode", "elem"),
            P(None, "elem"),
            P(None, "elem"),
            P("elem", None),
            P("elem"),
            P("mode", "elem", None),
            P("elem", None, None),
        ),
        out_specs=P(None, "mode", "elem"),
        check_vma=False,
    )
```
